256 devices in a mesh: img: 16 (over y_lo, z), gx: 4 (over y_hi, core), gy: 4 (over x).
Axes of the slice: x: 4, y: 4 (y_hi: 2, y_lo: 2; y = y_hi * 2 + y_lo), z: 8, core: 2. Of those that a mesh axis runs over, the one named last changes fastest.
Arguments:
- magnetization: float32 [16, 3, 16, 64, 512], P('img', None, None, 'gy', 'gx'), may hold values from -1 to 1, as said below
- lower_image: int32 [16], replicated, may hold values from 0 to 14, as said below
- image_weights: float32 [15], replicated, may hold values from 0.5 to 2
- regions: int32 [16, 64, 512], P(None, 'gy', 'gx'), may hold values from 0 to 7
- anisotropy: float32 [8], replicated, may hold values from 0.5 to 4
- damping: float32 [8], replicated, may hold values from 0.05 to 0.5
Outputs:
- evolved: float32 [16, 3, 16, 64, 512], P('img', None, None, 'gy', 'gx')
The draws below stay inside these ranges and needn't reach their ends.
Inputs may be any that keep to these rules, and one draw needn't show every extreme that they name: `lower_image`: lower_image_j is j - 1 or j; it is 0 for image 0 and 14 for the last image. `magnetization`: every cell holds a unit vector, and in every cell neighbouring images make an angle under 90 degrees.
All inputs are finite; a program needn't handle non-finite values.
Results may differ from the reference program's by a relative error of at most 0.000024.
Values sent between devices are 32-bit elements; how exact they have to be, the bound alone decides.
A program may use at most 64 MiB of HBM per device.

```python
import math
import jax
import jax.numpy as jnp
from jax import lax

NZ = 16
STEPS = 4
REGIONS = 8
IMAGES = 16
NX = 512
NY = 64


def draw_magnetization(key, part):
    base_key = jax.random.fold_in(key, 11)
    noise_key = jax.random.fold_in(key, 12)
    base = jax.random.normal(base_key, (3, NZ, NY, NX), jnp.float32)
    base = base * jax.lax.rsqrt(jnp.sum(base * base, axis=0, keepdims=True) + 1e-06)
    amplitude = 0.08 * (1.0 + 2.0 * jnp.arange(IMAGES, dtype=jnp.float32) / (IMAGES - 1))
    noise = jax.random.uniform(noise_key, (IMAGES, 3, NZ, NY, NX), jnp.float32, -1.0, 1.0)
    field = base[None] + amplitude[:, None, None, None, None] * noise
    return field * jax.lax.rsqrt(jnp.sum(field * field, axis=1, keepdims=True))


def draw_lower_image(key, part):
    step_back = jax.random.randint(jax.random.fold_in(key, 21), (IMAGES,), 0, 2)
    position = jnp.arange(IMAGES, dtype=jnp.int32)
    return jnp.clip(position - step_back, 0, IMAGES - 2).astype(jnp.int32)


def set_ends(values, stream_key, least, largest):
    place = [jax.random.randint(jax.random.fold_in(stream_key, axis), (), 0, length) for axis, length in enumerate(values.shape)]
    longest = values.shape.index(max(values.shape))
    neighbour = place[:longest] + [(place[longest] + 1) % values.shape[longest]] + place[longest + 1:]
    return values.at[tuple(place)].set(least).at[tuple(neighbour)].set(largest)


def setup_inputs(seed: int = 0) -> dict:
    arg_keys = jax.random.split(jax.random.key(seed), 7)
    return {
        "magnetization": draw_magnetization(jax.random.fold_in(arg_keys[6], 71), 0),
        "lower_image": draw_lower_image(jax.random.fold_in(arg_keys[6], 71), 0),
        "image_weights": jnp.clip(jnp.exp(jax.random.uniform(arg_keys[2], (IMAGES - 1,), jnp.float32, math.log(0.5), math.log(2.0))), 0.5, 2.0),
        "regions": set_ends(jax.random.randint(arg_keys[3], (NZ, NY, NX), 0, REGIONS), jax.random.fold_in(arg_keys[3], 1), 0, REGIONS - 1).astype(jnp.int32),
        "anisotropy": jnp.clip(jnp.exp(jax.random.uniform(arg_keys[4], (REGIONS,), jnp.float32, math.log(0.5), math.log(4.0))), 0.5, 4.0),
        "damping": jnp.clip(jnp.exp(jax.random.uniform(arg_keys[5], (REGIONS,), jnp.float32, math.log(0.05), math.log(0.5))), 0.05, 0.5),
    }


eps = 1e-06
time_step = 0.05

def normalize(field):
    return field * lax.rsqrt(field[..., 0, :, :, :] ** 2 + field[..., 1, :, :, :] ** 2 + field[..., 2, :, :, :] ** 2)[..., None, :, :, :]

def laplacian(field):
    plane = jnp.roll(field, 1, -1) + jnp.roll(field, -1, -1) + jnp.roll(field, 1, -2) + jnp.roll(field, -1, -2) - 4.0 * field
    upper = jnp.concatenate([field[..., 1:, :, :], field[..., -1:, :, :]], axis=-3)
    lower = jnp.concatenate([field[..., :1, :, :], field[..., :-1, :, :]], axis=-3)
    return plane + (upper + lower - 2.0 * field)

def torque_rate(field, lap, aniso, damp):
    mx, my, mz = (field[..., 0, :, :, :], field[..., 1, :, :, :], field[..., 2, :, :, :])
    hx, hy = (lap[..., 0, :, :, :], lap[..., 1, :, :, :])
    hz = lap[..., 2, :, :, :] + 2.0 * aniso * mz
    cx = my * hz - mz * hy
    cy = mz * hx - mx * hz
    cz = mx * hy - my * hx
    dx = my * cz - mz * cy
    dy = mz * cx - mx * cz
    dz = mx * cy - my * cx
    scale = -1.0 / (1.0 + damp * damp)
    return jnp.stack([scale * (cx + damp * dx), scale * (cy + damp * dy), scale * (cz + damp * dz)], axis=-4)

def evolve(field, aniso, damp):
    for step in range(STEPS):
        first = torque_rate(field, laplacian(field), aniso, damp)
        predicted = field + time_step * first
        second = torque_rate(predicted, laplacian(predicted), aniso, damp)
        field = normalize(field + 0.5 * time_step * (first + second))
    return field

def reference(magnetization, lower_image, image_weights, regions, anisotropy, damping):
    squares = lax.optimization_barrier(jnp.sum((magnetization[1:] - magnetization[:-1]) ** 2, axis=(1, 2, 3, 4)))
    lengths = jnp.concatenate([jnp.zeros((1,), jnp.float32), jnp.sqrt(squares + eps)])
    arc = jnp.cumsum(lengths)
    total = arc[-1]
    shares = jnp.concatenate([jnp.zeros((1,), jnp.float32), jnp.cumsum(image_weights)])
    target = shares / shares[-1]
    upper_image = lower_image + 1
    weight = jnp.clip((target * total - arc[lower_image]) / lengths[upper_image], -0.5, 1.5)
    weight = weight[:, None, None, None, None]
    start = normalize((1.0 - weight) * magnetization[lower_image] + weight * magnetization[upper_image])
    aniso = anisotropy[regions]
    damp = damping[regions]
    return lax.map(lambda field: evolve(field, aniso, damp), start)
```

```python
import jax
import jax.numpy as jnp
from jax import lax
from jax.experimental import pallas as pl
from jax.experimental.pallas import tpu as pltpu
from jax.sharding import PartitionSpec as P

STEPS = 4
EPS = 1e-06
TIME_STEP = 0.05
REGIONS = 8

ROWS = 16
RIM = 8
EXT = ROWS + 2 * RIM
HALF = ROWS // 2
LANES = 128
Y_LO = 2
MESH = pl.DeviceIdType.MESH


def roll_lanes(x, shift):
    shift = shift % LANES
    return x if shift == 0 else pltpu.roll(x, shift, axis=1)


def kernel(
    shape,
    mag, regions, lower, weights, anisotropy, damping,
    out,
    own, below, above, partner, reg,
    pack_own, pack_partner, rim_own, rim_partner, rim_start,
    main, main_next, main_coef, strip, strip_next, strip_coef, result,
    red_src, red_buf, line_src, line_buf,
    load_sem, out_sem, send_sem, recv_sem, red_sem,
):
    n_img, n_gx, n_gy = shape
    n_z = n_img // Y_LO
    img, gx, gy = lax.axis_index("img"), lax.axis_index("gx"), lax.axis_index("gy")
    y_lo, z = img // n_z, img % n_z
    left, right = lax.rem(gx + n_gx - 1, n_gx), lax.rem(gx + 1, n_gx)
    back, front = lax.rem(gy + n_gy - 1, n_gy), lax.rem(gy + 1, n_gy)
    prev, nxt = lax.rem(img + n_img - 1, n_img), lax.rem(img + 1, n_img)

    plane = Y_LO * n_gx * n_gy
    me_plane = (y_lo * n_gx + gx) * n_gy + gy

    def plane_peer(d):
        t = lax.rem(me_plane + d, plane)
        return ((t // (n_gx * n_gy)) * n_z + z, (t // n_gy) % n_gx, t % n_gy)

    def line_peer(d):
        return (y_lo * n_z + lax.rem(z + d, n_z), gx, gy)

    barrier = pltpu.get_barrier_semaphore()
    peers = [(prev, gx, gy), (nxt, gx, gy)]
    peers += [plane_peer(d) for d in range(1, plane)]
    peers += [line_peer(d) for d in range(1, n_z)]
    for peer in peers:
        pl.semaphore_signal(barrier, inc=1, device_id=peer, device_id_type=MESH)

    for y in range(ROWS):
        for h in range(2):
            pltpu.make_async_copy(
                mag.at[:, :, h, y, 0, :], own.at[RIM + y, h], load_sem.at[0]
            ).start()
            pltpu.make_async_copy(
                regions.at[:, h, y, 0, :], reg.at[RIM + y, h], load_sem.at[1]
            ).start()
    inner = pl.ds(RIM, ROWS)
    pltpu.make_async_copy(own.at[inner], own.at[inner], load_sem.at[0]).wait()
    pltpu.make_async_copy(reg.at[inner], reg.at[inner], load_sem.at[1]).wait()

    lane = lax.broadcasted_iota(jnp.int32, (8, LANES), 1)
    sub = lax.broadcasted_iota(jnp.int32, (8, LANES), 0)
    group = lane // RIM

    def packed(load, half, side):
        total = None
        for h in range(2):
            for k in range(8):
                at = h * 64 + k * 8
                piece = roll_lanes(load(RIM + half * 8 + k, h), at + (0 if side == 0 else RIM))
                total = piece if total is None else jnp.where(group == h * 8 + k, piece, total)
        return total

    for half in range(2):
        for side in range(2):
            for c in range(3):
                pack_own[side, half, c] = packed(lambda r, h: own[r, h, c], half, side)
            pack_own[side, half, 3] = packed(
                lambda r, h: reg[r, h].astype(jnp.float32), half, side
            )

    pl.semaphore_wait(barrier, len(peers))

    copies = []

    def send(src, dst, peer):
        n = len(copies)
        copy = pltpu.make_async_remote_copy(
            src_ref=src, dst_ref=dst, send_sem=send_sem.at[n], recv_sem=recv_sem.at[n],
            device_id=peer, device_id_type=MESH,
        )
        copy.start()
        copies.append(copy)
        return copy

    def send_rims(field, pack, rim):
        got = [
            send(field.at[pl.ds(RIM, RIM)], field.at[pl.ds(RIM + ROWS, RIM)], (img, gx, back)),
            send(field.at[pl.ds(RIM + HALF, RIM)], field.at[pl.ds(0, RIM)], (img, gx, front)),
            send(pack.at[1], rim.at[0, pl.ds(1, 2)], (img, right, gy)),
            send(pack.at[0], rim.at[1, pl.ds(1, 2)], (img, left, gy)),
            send(pack.at[1, 1], rim.at[0, 0], (img, right, front)),
            send(pack.at[1, 0], rim.at[0, 3], (img, right, back)),
            send(pack.at[0, 1], rim.at[1, 0], (img, left, front)),
            send(pack.at[0, 0], rim.at[1, 3], (img, left, back)),
        ]
        return got

    low, high = pl.ds(0, HALF), pl.ds(HALF, HALF)
    own_low, own_high = pl.ds(RIM, HALF), pl.ds(RIM + HALF, HALF)
    early = [
        send(own.at[own_low], below.at[low], (nxt, gx, gy)),
        send(own.at[own_high], above.at[high], (prev, gx, gy)),
    ]
    late = [
        send(own.at[own_high], below.at[high], (nxt, gx, gy)),
        send(own.at[own_low], above.at[low], (prev, gx, gy)),
    ]
    own_rims = send_rims(own, pack_own, rim_own)
    reg_rims = [
        send(reg.at[pl.ds(RIM, RIM)], reg.at[pl.ds(RIM + ROWS, RIM)], (img, gx, back)),
        send(reg.at[pl.ds(RIM + HALF, RIM)], reg.at[pl.ds(0, RIM)], (img, gx, front)),
    ]

    for copy in early:
        copy.wait_recv()

    def add_squares(r, sums):
        first, second = sums
        for h in range(2):
            for c in range(3):
                d = own[RIM + r, h, c] - below[r, h, c]
                first = first + d * d
                d = own[RIM + HALF + r, h, c] - above[HALF + r, h, c]
                second = second + d * d
        return first, second

    zero = jnp.zeros((8, LANES), jnp.float32)
    first, second = lax.fori_loop(0, HALF, add_squares, (zero, zero))
    row_lane = lax.broadcasted_iota(jnp.int32, (1, LANES), 1)
    partial = jnp.where(row_lane == img, jnp.sum(first), 0.0)
    partial = partial + jnp.where(row_lane == img + 1, jnp.sum(second), 0.0)
    red_src[...] = partial
    for d in range(1, plane):
        pltpu.make_async_remote_copy(
            src_ref=red_src, dst_ref=red_buf.at[d - 1], send_sem=red_sem.at[0],
            recv_sem=red_sem.at[1], device_id=plane_peer(d), device_id_type=MESH,
        ).start()

    for copy in late:
        copy.wait_recv()
    low_image = lower[img]
    use_above = jnp.full((8, LANES), low_image, jnp.int32) == img

    def choose(r, carry):
        for h in range(2):
            for c in range(3):
                partner[RIM + r, h, c] = jnp.where(use_above, above[r, h, c], below[r, h, c])
        return carry

    lax.fori_loop(0, ROWS, choose, 0)
    for half in range(2):
        for side in range(2):
            for c in range(3):
                pack_partner[side, half, c] = packed(
                    lambda r, h: partner[r, h, c], half, side
                )
    partner_rims = send_rims(partner, pack_partner, rim_partner)

    whole = pltpu.make_async_remote_copy(
        src_ref=red_buf, dst_ref=red_buf, send_sem=red_sem.at[0], recv_sem=red_sem.at[1],
        device_id=plane_peer(1), device_id_type=MESH,
    )
    whole.wait_recv()
    line_src[...] = red_src[...] + jnp.sum(red_buf[...], axis=0)
    for d in range(1, n_z):
        pltpu.make_async_remote_copy(
            src_ref=line_src, dst_ref=line_buf.at[d - 1], send_sem=red_sem.at[2],
            recv_sem=red_sem.at[3], device_id=line_peer(d), device_id_type=MESH,
        ).start()

    def assembled(i, k, h, load, load_rim, upper):
        at_a, at_b = h * 64 + k * 8, h * 64 + (7 - k) * 8
        group_a, group_b = (0, 3) if upper else (1, 2)
        a, b = load(i, h), load(EXT - 1 - i, h)
        v = roll_lanes(load_rim(1, group_b), 120 - at_b)
        v = jnp.where(lane < 120, roll_lanes(b, 120), v)
        v = jnp.where(lane < 96, roll_lanes(b, 72), v)
        v = jnp.where(lane < 72, roll_lanes(load_rim(0, group_b), 64 - at_b), v)
        v = jnp.where(lane < 64, roll_lanes(load_rim(1, group_a), 56 - at_a), v)
        v = jnp.where(lane < 56, roll_lanes(a, 56), v)
        v = jnp.where(lane < 32, roll_lanes(a, 8), v)
        return jnp.where(lane < 8, roll_lanes(load_rim(0, group_a), -at_a), v)

    def put_coef(ref, i, h, region):
        aniso = jnp.zeros((8, LANES), jnp.float32)
        damp = jnp.zeros((8, LANES), jnp.float32)
        for n in range(REGIONS):
            inside = region == n
            aniso = jnp.where(inside, anisotropy[n], aniso)
            damp = jnp.where(inside, damping[n], damp)
        ref[i, h, 0] = 2.0 * aniso
        ref[i, h, 1] = damp
        ref[i, h, 2] = -TIME_STEP / (1.0 + damp * damp)

    for copy in own_rims + reg_rims:
        copy.wait_recv()

    def main_coefs(r, carry):
        for h in range(2):
            put_coef(main_coef, r, h, reg[r, h])
        return carry

    lax.fori_loop(0, EXT, main_coefs, 0)
    for i in range(ROWS):
        for h in range(2):
            region = assembled(
                i, i % 8, h,
                lambda r, h: reg[r, h].astype(jnp.float32),
                lambda side, g: rim_own[side, g, 3],
                i < 8,
            )
            put_coef(strip_coef, i, h, region.astype(jnp.int32))

    share = jnp.float32(0.0)
    share_all = jnp.float32(0.0)
    for n in range(n_img - 1):
        share = share + jnp.where(n < img, weights[n], 0.0)
        share_all = share_all + weights[n]

    whole_line = pltpu.make_async_remote_copy(
        src_ref=line_buf, dst_ref=line_buf, send_sem=red_sem.at[2], recv_sem=red_sem.at[3],
        device_id=line_peer(1), device_id_type=MESH,
    )
    whole_line.wait_recv()
    squares = line_src[...] + jnp.sum(line_buf[...], axis=0)
    lengths = jnp.where(
        (row_lane >= 1) & (row_lane < n_img), jnp.sqrt(squares + EPS), 0.0
    )
    total = jnp.sum(lengths, axis=1, keepdims=True)
    low_row = jnp.full((1, LANES), low_image, jnp.int32)
    here = jnp.sum(jnp.where(row_lane <= low_row, lengths, 0.0), axis=1, keepdims=True)
    gap = jnp.sum(jnp.where(row_lane == low_row + 1, lengths, 0.0), axis=1, keepdims=True)
    aim = jnp.full((1, 1), share, jnp.float32) / jnp.full((1, 1), share_all, jnp.float32)
    weight = jnp.clip((aim * total - here) / gap, -0.5, 1.5)
    weight = jnp.broadcast_to(weight, (8, LANES))
    own_part = jnp.where(use_above, 1.0 - weight, weight)
    partner_part = jnp.where(use_above, weight, 1.0 - weight)

    def unit(v):
        scale = lax.rsqrt(v[0] * v[0] + v[1] * v[1] + v[2] * v[2])
        return [x * scale for x in v]

    for copy in partner_rims:
        copy.wait_recv()

    def start_main(r, carry):
        for h in range(2):
            v = unit([own_part * own[r, h, c] + partner_part * partner[r, h, c] for c in range(3)])
            for c in range(3):
                main[r, h, c] = v[c]
        return carry

    lax.fori_loop(0, EXT, start_main, 0)
    for side in range(2):
        for g in range(4):
            v = unit([
                own_part * rim_own[side, g, c] + partner_part * rim_partner[side, g, c]
                for c in range(3)
            ])
            for c in range(3):
                rim_start[side, g, c] = v[c]
    for i in range(ROWS):
        for h in range(2):
            for c in range(3):
                strip[i, h, c] = assembled(
                    i, i % 8, h,
                    lambda r, h: main[r, h, c],
                    lambda side, g: rim_start[side, g, c],
                    i < 8,
                )

    def fold(ref):
        for h in range(2):
            for c in range(3):
                ref[ROWS, h, c] = roll_lanes(ref[ROWS - 1, h, c], 64)

    fold(strip)

    first_z, last_z = sub == 0, sub == 7

    def moved(field, coef, r):
        m = [[field[r, h, c] for c in range(3)] for h in range(2)]
        moves = []
        for h in range(2):
            lap = []
            for c in range(3):
                here, other = m[h][c], m[1 - h][c]
                if h == 0:
                    edge = jnp.where(first_z, here, pltpu.roll(other, 1, axis=0))
                else:
                    edge = jnp.where(last_z, here, pltpu.roll(other, 7, axis=0))
                near = roll_lanes(here, 1) + roll_lanes(here, LANES - 1)
                near = near + (field[r - 1, h, c] + field[r + 1, h, c])
                lap.append(near + (other + edge) - 6.0 * here)
            mx, my, mz = m[h]
            twice_aniso, damp, scale = coef[r, h, 0], coef[r, h, 1], coef[r, h, 2]
            hx, hy, hz = lap[0], lap[1], lap[2] + twice_aniso * mz
            gx_ = hx + damp * (my * hz - mz * hy)
            gy_ = hy + damp * (mz * hx - mx * hz)
            gz_ = hz + damp * (mx * hy - my * hx)
            moves.append([
                scale * (my * gz_ - mz * gy_),
                scale * (mz * gx_ - mx * gz_),
                scale * (mx * gy_ - my * gx_),
            ])
        return m, moves

    def predict(field, nextf, coef, r):
        m, moves = moved(field, coef, r)
        for h in range(2):
            for c in range(3):
                nextf[r, h, c] = m[h][c] + moves[h][c]

    def correct(field, nextf, coef, r):
        p, moves = moved(nextf, coef, r)
        new = []
        for h in range(2):
            new.append(unit([(field[r, h, c] + p[h][c]) + moves[h][c] for c in range(3)]))
        return new

    def run(lo, hi, fn):
        def step(r, carry):
            fn(r)
            return carry

        lax.fori_loop(lo, hi, step, 0)

    def correct_to(field, nextf, coef):
        def fn(r):
            new = correct(field, nextf, coef, r)
            for h in range(2):
                for c in range(3):
                    field[r, h, c] = new[h][c]

        return fn

    for step in range(STEPS):
        k = 2 * step + 1
        run(k, EXT - k, lambda r: predict(main, main_next, main_coef, r))
        run(k, ROWS, lambda r: predict(strip, strip_next, strip_coef, r))
        fold(strip_next)
        k = k + 1
        run(k, ROWS, correct_to(strip, strip_next, strip_coef))
        if step < STEPS - 1:
            fold(strip)
            run(k, EXT - k, correct_to(main, main_next, main_coef))

    def finish(base, strip_row):
        def fn(r):
            new = correct(main, main_next, main_coef, r)
            for h in range(2):
                for c in range(3):
                    s = strip[strip_row(r), h, c]
                    v = jnp.where(lane < 8, roll_lanes(s, -(base + 8)), new[h][c])
                    v = jnp.where(lane >= 120, roll_lanes(s, 72 - base), v)
                    result[r - RIM, h, c] = v

        return fn

    run(RIM, ROWS, finish(0, lambda r: r))
    run(ROWS, EXT - RIM, finish(64, lambda r: EXT - 1 - r))
    for y in range(ROWS):
        for h in range(2):
            pltpu.make_async_copy(
                result.at[y, h], out.at[:, :, h, y, 0, :], out_sem
            ).start()
    for copy in copies:
        copy.wait_send()
    whole.wait_send()
    whole_line.wait_send()
    pltpu.make_async_copy(result, result, out_sem).wait()


def body(shape, magnetization, lower_image, image_weights, regions, anisotropy, damping):
    n_img, n_gx, n_gy = shape
    plane = Y_LO * n_gx * n_gy
    f32 = jnp.float32
    tile = (8, LANES)
    smem = pl.BlockSpec(memory_space=pltpu.SMEM)
    anywhere = pl.BlockSpec(memory_space=pl.ANY)
    n_copies = 4 + 8 + 2 + 8
    out = pl.pallas_call(
        lambda *refs: kernel(shape, *refs),
        out_shape=jax.ShapeDtypeStruct((3, 8, 2, ROWS, 1, LANES), f32),
        in_specs=[anywhere, anywhere, smem, smem, smem, smem],
        out_specs=anywhere,
        scratch_shapes=[
            pltpu.VMEM((EXT, 2, 3) + tile, f32),
            pltpu.VMEM((ROWS, 2, 3) + tile, f32),
            pltpu.VMEM((ROWS, 2, 3) + tile, f32),
            pltpu.VMEM((EXT, 2, 3) + tile, f32),
            pltpu.VMEM((EXT, 2) + tile, jnp.int32),
            pltpu.VMEM((2, 2, 4) + tile, f32),
            pltpu.VMEM((2, 2, 3) + tile, f32),
            pltpu.VMEM((2, 4, 4) + tile, f32),
            pltpu.VMEM((2, 4, 3) + tile, f32),
            pltpu.VMEM((2, 4, 3) + tile, f32),
            pltpu.VMEM((EXT, 2, 3) + tile, f32),
            pltpu.VMEM((EXT, 2, 3) + tile, f32),
            pltpu.VMEM((EXT, 2, 3) + tile, f32),
            pltpu.VMEM((ROWS + 1, 2, 3) + tile, f32),
            pltpu.VMEM((ROWS + 1, 2, 3) + tile, f32),
            pltpu.VMEM((ROWS, 2, 3) + tile, f32),
            pltpu.VMEM((ROWS, 2, 3) + tile, f32),
            pltpu.VMEM((1, LANES), f32),
            pltpu.VMEM((plane - 1, 1, LANES), f32),
            pltpu.VMEM((1, LANES), f32),
            pltpu.VMEM((n_img // Y_LO - 1, 1, LANES), f32),
            pltpu.SemaphoreType.DMA((2,)),
            pltpu.SemaphoreType.DMA,
            pltpu.SemaphoreType.DMA((n_copies,)),
            pltpu.SemaphoreType.DMA((n_copies,)),
            pltpu.SemaphoreType.DMA((4,)),
        ],
        compiler_params=pltpu.CompilerParams(collective_id=0, has_side_effects=True),
    )(
        magnetization.reshape(3, 8, 2, ROWS, 1, LANES),
        regions.reshape(8, 2, ROWS, 1, LANES),
        lower_image,
        image_weights,
        anisotropy,
        damping,
    )
    return out.reshape(magnetization.shape)


def solution(mesh):
    placed = (P("img", None, None, "gy", "gx"), P(), P(), P(None, "gy", "gx"), P(), P())
    shape = (mesh.shape["img"], mesh.shape["gx"], mesh.shape["gy"])
    return jax.shard_map(
        lambda *args: body(shape, *args),
        mesh=mesh,
        in_specs=placed,
        out_specs=P("img", None, None, "gy", "gx"),
        check_vma=False,
    )
```

```python
import jax
import jax.numpy as jnp
from jax import lax
from jax.experimental import pallas as pl
from jax.experimental.pallas import tpu as pltpu
from jax.sharding import PartitionSpec as P

STEPS = 4
EPS = 1e-06
TIME_STEP = 0.05
REGIONS = 8

ROWS = 16
RIM = 8
EXT = ROWS + 2 * RIM
HALF = ROWS // 2
LANES = 128
Y_LO = 2
MESH = pl.DeviceIdType.MESH


def roll_lanes(x, shift):
    shift = shift % LANES
    return x if shift == 0 else pltpu.roll(x, shift, axis=1)


def kernel(
    shape,
    mag, regions, lower, weights, anisotropy, damping,
    out,
    own, below, above, partner, reg,
    pack_own, pack_partner, rim_own, rim_partner, rim_start,
    main, main_next, main_coef, strip, strip_next, strip_coef, result,
    red_src, red_buf, line_src, line_buf,
    load_sem, out_sem, send_sem, recv_sem, red_sem,
):
    n_img, n_gx, n_gy = shape
    n_z = n_img // Y_LO
    img, gx, gy = lax.axis_index("img"), lax.axis_index("gx"), lax.axis_index("gy")
    y_lo, z = img // n_z, img % n_z
    left, right = lax.rem(gx + n_gx - 1, n_gx), lax.rem(gx + 1, n_gx)
    back, front = lax.rem(gy + n_gy - 1, n_gy), lax.rem(gy + 1, n_gy)
    prev, nxt = lax.rem(img + n_img - 1, n_img), lax.rem(img + 1, n_img)

    plane = Y_LO * n_gx * n_gy
    me_plane = (y_lo * n_gx + gx) * n_gy + gy

    def plane_peer(d):
        t = lax.rem(me_plane + d, plane)
        return ((t // (n_gx * n_gy)) * n_z + z, (t // n_gy) % n_gx, t % n_gy)

    def line_peer(d):
        return (y_lo * n_z + lax.rem(z + d, n_z), gx, gy)

    barrier = pltpu.get_barrier_semaphore()
    peers = [(prev, gx, gy), (nxt, gx, gy)]
    peers += [plane_peer(d) for d in range(1, plane)]
    peers += [line_peer(d) for d in range(1, n_z)]
    for peer in peers:
        pl.semaphore_signal(barrier, inc=1, device_id=peer, device_id_type=MESH)

    for y in range(ROWS):
        for h in range(2):
            pltpu.make_async_copy(
                mag.at[:, :, h, y, 0, :], own.at[RIM + y, h], load_sem.at[0]
            ).start()
            pltpu.make_async_copy(
                regions.at[:, h, y, 0, :], reg.at[RIM + y, h], load_sem.at[1]
            ).start()
    inner = pl.ds(RIM, ROWS)
    pltpu.make_async_copy(own.at[inner], own.at[inner], load_sem.at[0]).wait()
    pltpu.make_async_copy(reg.at[inner], reg.at[inner], load_sem.at[1]).wait()

    lane = lax.broadcasted_iota(jnp.int32, (8, LANES), 1)
    sub = lax.broadcasted_iota(jnp.int32, (8, LANES), 0)
    group = lane // RIM

    def packed(load, half, side):
        total = None
        for h in range(2):
            for k in range(8):
                at = h * 64 + k * 8
                piece = roll_lanes(load(RIM + half * 8 + k, h), at + (0 if side == 0 else RIM))
                total = piece if total is None else jnp.where(group == h * 8 + k, piece, total)
        return total

    for half in range(2):
        for side in range(2):
            for c in range(3):
                pack_own[side, half, c] = packed(lambda r, h: own[r, h, c], half, side)
            pack_own[side, half, 3] = packed(
                lambda r, h: reg[r, h].astype(jnp.float32), half, side
            )

    pl.semaphore_wait(barrier, len(peers))

    copies = []

    def send(src, dst, peer):
        n = len(copies)
        copy = pltpu.make_async_remote_copy(
            src_ref=src, dst_ref=dst, send_sem=send_sem.at[n], recv_sem=recv_sem.at[n],
            device_id=peer, device_id_type=MESH,
        )
        copy.start()
        copies.append(copy)
        return copy

    def send_rims(field, pack, rim):
        got = [
            send(field.at[pl.ds(RIM, RIM)], field.at[pl.ds(RIM + ROWS, RIM)], (img, gx, back)),
            send(field.at[pl.ds(RIM + HALF, RIM)], field.at[pl.ds(0, RIM)], (img, gx, front)),
            send(pack.at[1], rim.at[0, pl.ds(1, 2)], (img, right, gy)),
            send(pack.at[0], rim.at[1, pl.ds(1, 2)], (img, left, gy)),
            send(pack.at[1, 1], rim.at[0, 0], (img, right, front)),
            send(pack.at[1, 0], rim.at[0, 3], (img, right, back)),
            send(pack.at[0, 1], rim.at[1, 0], (img, left, front)),
            send(pack.at[0, 0], rim.at[1, 3], (img, left, back)),
        ]
        return got

    low, high = pl.ds(0, HALF), pl.ds(HALF, HALF)
    own_low, own_high = pl.ds(RIM, HALF), pl.ds(RIM + HALF, HALF)
    early = [
        send(own.at[own_low], below.at[low], (nxt, gx, gy)),
        send(own.at[own_high], above.at[high], (prev, gx, gy)),
    ]
    late = [
        send(own.at[own_high], below.at[high], (nxt, gx, gy)),
        send(own.at[own_low], above.at[low], (prev, gx, gy)),
    ]
    own_rims = send_rims(own, pack_own, rim_own)
    reg_rims = [
        send(reg.at[pl.ds(RIM, RIM)], reg.at[pl.ds(RIM + ROWS, RIM)], (img, gx, back)),
        send(reg.at[pl.ds(RIM + HALF, RIM)], reg.at[pl.ds(0, RIM)], (img, gx, front)),
    ]

    for copy in early:
        copy.wait_recv()

    def add_squares(r, sums):
        first, second = sums
        for h in range(2):
            for c in range(3):
                d = own[RIM + r, h, c] - below[r, h, c]
                first = first + d * d
                d = own[RIM + HALF + r, h, c] - above[HALF + r, h, c]
                second = second + d * d
        return first, second

    zero = jnp.zeros((8, LANES), jnp.float32)
    first, second = lax.fori_loop(0, HALF, add_squares, (zero, zero))
    row_lane = lax.broadcasted_iota(jnp.int32, (1, LANES), 1)
    partial = jnp.where(row_lane == img, jnp.sum(first), 0.0)
    partial = partial + jnp.where(row_lane == img + 1, jnp.sum(second), 0.0)
    red_src[...] = partial
    for d in range(1, plane):
        pltpu.make_async_remote_copy(
            src_ref=red_src, dst_ref=red_buf.at[d - 1], send_sem=red_sem.at[0],
            recv_sem=red_sem.at[1], device_id=plane_peer(d), device_id_type=MESH,
        ).start()

    for copy in late:
        copy.wait_recv()
    low_image = lower[img]
    use_above = jnp.full((8, LANES), low_image, jnp.int32) == img

    def choose(r, carry):
        for h in range(2):
            for c in range(3):
                partner[RIM + r, h, c] = jnp.where(use_above, above[r, h, c], below[r, h, c])
        return carry

    lax.fori_loop(0, ROWS, choose, 0)
    for half in range(2):
        for side in range(2):
            for c in range(3):
                pack_partner[side, half, c] = packed(
                    lambda r, h: partner[r, h, c], half, side
                )
    partner_rims = send_rims(partner, pack_partner, rim_partner)

    whole = pltpu.make_async_remote_copy(
        src_ref=red_buf, dst_ref=red_buf, send_sem=red_sem.at[0], recv_sem=red_sem.at[1],
        device_id=plane_peer(1), device_id_type=MESH,
    )
    whole.wait_recv()
    line_src[...] = red_src[...] + jnp.sum(red_buf[...], axis=0)
    for d in range(1, n_z):
        pltpu.make_async_remote_copy(
            src_ref=line_src, dst_ref=line_buf.at[d - 1], send_sem=red_sem.at[2],
            recv_sem=red_sem.at[3], device_id=line_peer(d), device_id_type=MESH,
        ).start()

    def assembled(i, k, h, load, load_rim, upper):
        at_a, at_b = h * 64 + k * 8, h * 64 + (7 - k) * 8
        group_a, group_b = (0, 3) if upper else (1, 2)
        a, b = load(i, h), load(EXT - 1 - i, h)
        v = roll_lanes(load_rim(1, group_b), 120 - at_b)
        v = jnp.where(lane < 120, roll_lanes(b, 120), v)
        v = jnp.where(lane < 96, roll_lanes(b, 72), v)
        v = jnp.where(lane < 72, roll_lanes(load_rim(0, group_b), 64 - at_b), v)
        v = jnp.where(lane < 64, roll_lanes(load_rim(1, group_a), 56 - at_a), v)
        v = jnp.where(lane < 56, roll_lanes(a, 56), v)
        v = jnp.where(lane < 32, roll_lanes(a, 8), v)
        return jnp.where(lane < 8, roll_lanes(load_rim(0, group_a), -at_a), v)

    def put_coef(ref, i, h, region):
        aniso = jnp.zeros((8, LANES), jnp.float32)
        damp = jnp.zeros((8, LANES), jnp.float32)
        for n in range(REGIONS):
            inside = region == n
            aniso = jnp.where(inside, anisotropy[n], aniso)
            damp = jnp.where(inside, damping[n], damp)
        ref[i, h, 0] = 2.0 * aniso
        ref[i, h, 1] = damp
        ref[i, h, 2] = -TIME_STEP / (1.0 + damp * damp)

    for copy in own_rims + reg_rims:
        copy.wait_recv()

    def main_coefs(r, carry):
        for h in range(2):
            put_coef(main_coef, r, h, reg[r, h])
        return carry

    lax.fori_loop(0, EXT, main_coefs, 0)
    for i in range(ROWS):
        for h in range(2):
            region = assembled(
                i, i % 8, h,
                lambda r, h: reg[r, h].astype(jnp.float32),
                lambda side, g: rim_own[side, g, 3],
                i < 8,
            )
            put_coef(strip_coef, i, h, region.astype(jnp.int32))

    share = jnp.float32(0.0)
    share_all = jnp.float32(0.0)
    for n in range(n_img - 1):
        share = share + jnp.where(n < img, weights[n], 0.0)
        share_all = share_all + weights[n]

    whole_line = pltpu.make_async_remote_copy(
        src_ref=line_buf, dst_ref=line_buf, send_sem=red_sem.at[2], recv_sem=red_sem.at[3],
        device_id=line_peer(1), device_id_type=MESH,
    )
    whole_line.wait_recv()
    squares = line_src[...] + jnp.sum(line_buf[...], axis=0)
    lengths = jnp.where(
        (row_lane >= 1) & (row_lane < n_img), jnp.sqrt(squares + EPS), 0.0
    )
    total = jnp.sum(lengths, axis=1, keepdims=True)
    low_row = jnp.full((1, LANES), low_image, jnp.int32)
    here = jnp.sum(jnp.where(row_lane <= low_row, lengths, 0.0), axis=1, keepdims=True)
    gap = jnp.sum(jnp.where(row_lane == low_row + 1, lengths, 0.0), axis=1, keepdims=True)
    aim = jnp.full((1, 1), share, jnp.float32) / jnp.full((1, 1), share_all, jnp.float32)
    weight = jnp.clip((aim * total - here) / gap, -0.5, 1.5)
    weight = jnp.broadcast_to(weight, (8, LANES))
    own_part = jnp.where(use_above, 1.0 - weight, weight)
    partner_part = jnp.where(use_above, weight, 1.0 - weight)

    def unit(v):
        scale = lax.rsqrt(v[0] * v[0] + v[1] * v[1] + v[2] * v[2])
        return [x * scale for x in v]

    for copy in partner_rims:
        copy.wait_recv()

    def start_main(r, carry):
        for h in range(2):
            v = unit([own_part * own[r, h, c] + partner_part * partner[r, h, c] for c in range(3)])
            for c in range(3):
                main[r, h, c] = v[c]
        return carry

    lax.fori_loop(0, EXT, start_main, 0)
    for side in range(2):
        for g in range(4):
            v = unit([
                own_part * rim_own[side, g, c] + partner_part * rim_partner[side, g, c]
                for c in range(3)
            ])
            for c in range(3):
                rim_start[side, g, c] = v[c]
    for i in range(ROWS):
        for h in range(2):
            for c in range(3):
                strip[i, h, c] = assembled(
                    i, i % 8, h,
                    lambda r, h: main[r, h, c],
                    lambda side, g: rim_start[side, g, c],
                    i < 8,
                )

    def fold(ref):
        for h in range(2):
            for c in range(3):
                ref[ROWS, h, c] = roll_lanes(ref[ROWS - 1, h, c], 64)

    fold(strip)

    first_z, last_z = sub == 0, sub == 7

    def moved(field, coef, r):
        m = [[field[r, h, c] for c in range(3)] for h in range(2)]
        moves = []
        for h in range(2):
            lap = []
            for c in range(3):
                here, other = m[h][c], m[1 - h][c]
                if h == 0:
                    edge = jnp.where(first_z, here, pltpu.roll(other, 1, axis=0))
                else:
                    edge = jnp.where(last_z, here, pltpu.roll(other, 7, axis=0))
                near = roll_lanes(here, 1) + roll_lanes(here, LANES - 1)
                near = near + (field[r - 1, h, c] + field[r + 1, h, c])
                lap.append(near + (other + edge) - 6.0 * here)
            mx, my, mz = m[h]
            twice_aniso, damp, scale = coef[r, h, 0], coef[r, h, 1], coef[r, h, 2]
            hx, hy, hz = lap[0], lap[1], lap[2] + twice_aniso * mz
            gx_ = hx + damp * (my * hz - mz * hy)
            gy_ = hy + damp * (mz * hx - mx * hz)
            gz_ = hz + damp * (mx * hy - my * hx)
            moves.append([
                scale * (my * gz_ - mz * gy_),
                scale * (mz * gx_ - mx * gz_),
                scale * (mx * gy_ - my * gx_),
            ])
        return m, moves

    def predict(field, nextf, coef, r):
        m, moves = moved(field, coef, r)
        for h in range(2):
            for c in range(3):
                nextf[r, h, c] = m[h][c] + moves[h][c]

    def correct(field, nextf, coef, r):
        p, moves = moved(nextf, coef, r)
        new = []
        for h in range(2):
            new.append(unit([(field[r, h, c] + p[h][c]) + moves[h][c] for c in range(3)]))
        return new

    def run(lo, hi, fn):
        def step(r, carry):
            fn(r)
            return carry

        lax.fori_loop(lo, hi, step, 0, unroll=4)

    def correct_to(field, nextf, coef):
        def fn(r):
            new = correct(field, nextf, coef, r)
            for h in range(2):
                for c in range(3):
                    field[r, h, c] = new[h][c]

        return fn

    for step in range(STEPS):
        k = 2 * step + 1
        run(k, EXT - k, lambda r: predict(main, main_next, main_coef, r))
        run(k, ROWS, lambda r: predict(strip, strip_next, strip_coef, r))
        fold(strip_next)
        k = k + 1
        run(k, ROWS, correct_to(strip, strip_next, strip_coef))
        if step < STEPS - 1:
            fold(strip)
            run(k, EXT - k, correct_to(main, main_next, main_coef))

    def finish(base, strip_row):
        def fn(r):
            new = correct(main, main_next, main_coef, r)
            for h in range(2):
                for c in range(3):
                    s = strip[strip_row(r), h, c]
                    v = jnp.where(lane < 8, roll_lanes(s, -(base + 8)), new[h][c])
                    v = jnp.where(lane >= 120, roll_lanes(s, 72 - base), v)
                    result[r - RIM, h, c] = v

        return fn

    run(RIM, ROWS, finish(0, lambda r: r))
    run(ROWS, EXT - RIM, finish(64, lambda r: EXT - 1 - r))
    for y in range(ROWS):
        for h in range(2):
            pltpu.make_async_copy(
                result.at[y, h], out.at[:, :, h, y, 0, :], out_sem
            ).start()
    for copy in copies:
        copy.wait_send()
    whole.wait_send()
    whole_line.wait_send()
    pltpu.make_async_copy(result, result, out_sem).wait()


def body(shape, magnetization, lower_image, image_weights, regions, anisotropy, damping):
    n_img, n_gx, n_gy = shape
    plane = Y_LO * n_gx * n_gy
    f32 = jnp.float32
    tile = (8, LANES)
    smem = pl.BlockSpec(memory_space=pltpu.SMEM)
    anywhere = pl.BlockSpec(memory_space=pl.ANY)
    n_copies = 4 + 8 + 2 + 8
    out = pl.pallas_call(
        lambda *refs: kernel(shape, *refs),
        out_shape=jax.ShapeDtypeStruct((3, 8, 2, ROWS, 1, LANES), f32),
        in_specs=[anywhere, anywhere, smem, smem, smem, smem],
        out_specs=anywhere,
        scratch_shapes=[
            pltpu.VMEM((EXT, 2, 3) + tile, f32),
            pltpu.VMEM((ROWS, 2, 3) + tile, f32),
            pltpu.VMEM((ROWS, 2, 3) + tile, f32),
            pltpu.VMEM((EXT, 2, 3) + tile, f32),
            pltpu.VMEM((EXT, 2) + tile, jnp.int32),
            pltpu.VMEM((2, 2, 4) + tile, f32),
            pltpu.VMEM((2, 2, 3) + tile, f32),
            pltpu.VMEM((2, 4, 4) + tile, f32),
            pltpu.VMEM((2, 4, 3) + tile, f32),
            pltpu.VMEM((2, 4, 3) + tile, f32),
            pltpu.VMEM((EXT, 2, 3) + tile, f32),
            pltpu.VMEM((EXT, 2, 3) + tile, f32),
            pltpu.VMEM((EXT, 2, 3) + tile, f32),
            pltpu.VMEM((ROWS + 1, 2, 3) + tile, f32),
            pltpu.VMEM((ROWS + 1, 2, 3) + tile, f32),
            pltpu.VMEM((ROWS, 2, 3) + tile, f32),
            pltpu.VMEM((ROWS, 2, 3) + tile, f32),
            pltpu.VMEM((1, LANES), f32),
            pltpu.VMEM((plane - 1, 1, LANES), f32),
            pltpu.VMEM((1, LANES), f32),
            pltpu.VMEM((n_img // Y_LO - 1, 1, LANES), f32),
            pltpu.SemaphoreType.DMA((2,)),
            pltpu.SemaphoreType.DMA,
            pltpu.SemaphoreType.DMA((n_copies,)),
            pltpu.SemaphoreType.DMA((n_copies,)),
            pltpu.SemaphoreType.DMA((4,)),
        ],
        compiler_params=pltpu.CompilerParams(collective_id=0, has_side_effects=True),
    )(
        magnetization.reshape(3, 8, 2, ROWS, 1, LANES),
        regions.reshape(8, 2, ROWS, 1, LANES),
        lower_image,
        image_weights,
        anisotropy,
        damping,
    )
    return out.reshape(magnetization.shape)


def solution(mesh):
    placed = (P("img", None, None, "gy", "gx"), P(), P(), P(None, "gy", "gx"), P(), P())
    shape = (mesh.shape["img"], mesh.shape["gx"], mesh.shape["gy"])
    return jax.shard_map(
        lambda *args: body(shape, *args),
        mesh=mesh,
        in_specs=placed,
        out_specs=P("img", None, None, "gy", "gx"),
        check_vma=False,
    )
```

```python
import jax
import jax.numpy as jnp
from jax import lax
from jax.experimental import pallas as pl
from jax.experimental.pallas import tpu as pltpu
from jax.sharding import PartitionSpec as P

STEPS = 4
EPS = 1e-06
TIME_STEP = 0.05
REGIONS = 8

ROWS = 16
RIM = 8
EXT = ROWS + 2 * RIM
HALF = ROWS // 2
LANES = 128
Y_LO = 2
MESH = pl.DeviceIdType.MESH


def roll_lanes(x, shift):
    shift = shift % LANES
    return x if shift == 0 else pltpu.roll(x, shift, axis=1)


def kernel(
    shape,
    mag, regions, lower, weights, anisotropy, damping,
    out,
    own, below, above, partner, reg,
    pack_own, pack_partner, rim_own, rim_partner, rim_start,
    main, main_next, main_coef, strip, strip_next, strip_coef, near, result,
    red_src, red_buf, line_src, line_buf,
    load_sem, out_sem, image_sem, send_sem, recv_sem, red_sem,
):
    n_img, n_gx, n_gy = shape
    n_z = n_img // Y_LO
    img, gx, gy = lax.axis_index("img"), lax.axis_index("gx"), lax.axis_index("gy")
    y_lo, z = img // n_z, img % n_z
    left, right = lax.rem(gx + n_gx - 1, n_gx), lax.rem(gx + 1, n_gx)
    back, front = lax.rem(gy + n_gy - 1, n_gy), lax.rem(gy + 1, n_gy)
    prev, nxt = lax.rem(img + n_img - 1, n_img), lax.rem(img + 1, n_img)

    plane = Y_LO * n_gx * n_gy
    me_plane = (y_lo * n_gx + gx) * n_gy + gy

    def plane_peer(d):
        t = lax.rem(me_plane + d, plane)
        return ((t // (n_gx * n_gy)) * n_z + z, (t // n_gy) % n_gx, t % n_gy)

    def line_peer(d):
        return (y_lo * n_z + lax.rem(z + d, n_z), gx, gy)

    barrier = pltpu.get_barrier_semaphore()
    peers = [(prev, gx, gy), (nxt, gx, gy)]
    peers += [plane_peer(d) for d in range(1, plane)]
    peers += [line_peer(d) for d in range(1, n_z)]
    for peer in peers:
        pl.semaphore_signal(barrier, inc=1, device_id=peer, device_id_type=MESH)

    pl.semaphore_wait(barrier, len(peers))

    to_next, to_prev = (nxt, gx, gy), (prev, gx, gy)

    def send_image(n, rows, field, peer):
        for y in rows:
            for h in range(2):
                pltpu.make_async_remote_copy(
                    src_ref=mag.at[:, :, h, y, 0, :], dst_ref=field.at[y, h],
                    send_sem=image_sem.at[0, n], recv_sem=image_sem.at[1, n],
                    device_id=peer, device_id_type=MESH,
                ).start()
        part = field.at[pl.ds(rows[0], len(rows))]
        return pltpu.make_async_remote_copy(
            src_ref=part, dst_ref=part, send_sem=image_sem.at[0, n],
            recv_sem=image_sem.at[1, n], device_id=peer, device_id_type=MESH,
        )

    low_rows, high_rows = list(range(HALF)), list(range(HALF, ROWS))
    early = [send_image(0, low_rows, below, to_next), send_image(1, high_rows, above, to_prev)]

    for y in range(ROWS):
        for h in range(2):
            pltpu.make_async_copy(
                mag.at[:, :, h, y, 0, :], own.at[RIM + y, h], load_sem.at[0]
            ).start()
    late = [send_image(2, high_rows, below, to_next), send_image(3, low_rows, above, to_prev)]
    for y in range(ROWS):
        for h in range(2):
            pltpu.make_async_copy(
                regions.at[:, h, y, 0, :], reg.at[RIM + y, h], load_sem.at[1]
            ).start()
    inner = pl.ds(RIM, ROWS)
    pltpu.make_async_copy(own.at[inner], own.at[inner], load_sem.at[0]).wait()
    pltpu.make_async_copy(reg.at[inner], reg.at[inner], load_sem.at[1]).wait()

    lane = lax.broadcasted_iota(jnp.int32, (8, LANES), 1)
    sub = lax.broadcasted_iota(jnp.int32, (8, LANES), 0)
    group = lane // RIM

    def packed(load, half, side):
        total = None
        for h in range(2):
            for k in range(8):
                at = h * 64 + k * 8
                piece = roll_lanes(load(RIM + half * 8 + k, h), at + (0 if side == 0 else RIM))
                total = piece if total is None else jnp.where(group == h * 8 + k, piece, total)
        return total

    for half in range(2):
        for side in range(2):
            for c in range(3):
                pack_own[side, half, c] = packed(lambda r, h: own[r, h, c], half, side)
            pack_own[side, half, 3] = packed(
                lambda r, h: reg[r, h].astype(jnp.float32), half, side
            )

    copies = []

    def send(src, dst, peer):
        n = len(copies)
        copy = pltpu.make_async_remote_copy(
            src_ref=src, dst_ref=dst, send_sem=send_sem.at[n], recv_sem=recv_sem.at[n],
            device_id=peer, device_id_type=MESH,
        )
        copy.start()
        copies.append(copy)
        return copy

    def send_rims(field, pack, rim):
        got = [
            send(field.at[pl.ds(RIM, RIM)], field.at[pl.ds(RIM + ROWS, RIM)], (img, gx, back)),
            send(field.at[pl.ds(RIM + HALF, RIM)], field.at[pl.ds(0, RIM)], (img, gx, front)),
            send(pack.at[1], rim.at[0, pl.ds(1, 2)], (img, right, gy)),
            send(pack.at[0], rim.at[1, pl.ds(1, 2)], (img, left, gy)),
            send(pack.at[1, 1], rim.at[0, 0], (img, right, front)),
            send(pack.at[1, 0], rim.at[0, 3], (img, right, back)),
            send(pack.at[0, 1], rim.at[1, 0], (img, left, front)),
            send(pack.at[0, 0], rim.at[1, 3], (img, left, back)),
        ]
        return got

    own_rims = send_rims(own, pack_own, rim_own)
    reg_rims = [
        send(reg.at[pl.ds(RIM, RIM)], reg.at[pl.ds(RIM + ROWS, RIM)], (img, gx, back)),
        send(reg.at[pl.ds(RIM + HALF, RIM)], reg.at[pl.ds(0, RIM)], (img, gx, front)),
    ]

    for copy in early:
        copy.wait_recv()

    def add_squares(r, sums):
        first, second = sums
        for h in range(2):
            for c in range(3):
                d = own[RIM + r, h, c] - below[r, h, c]
                first = first + d * d
                d = own[RIM + HALF + r, h, c] - above[HALF + r, h, c]
                second = second + d * d
        return first, second

    zero = jnp.zeros((8, LANES), jnp.float32)
    first, second = lax.fori_loop(0, HALF, add_squares, (zero, zero))
    row_lane = lax.broadcasted_iota(jnp.int32, (1, LANES), 1)
    partial = jnp.where(row_lane == img, jnp.sum(first), 0.0)
    partial = partial + jnp.where(row_lane == img + 1, jnp.sum(second), 0.0)
    red_src[...] = partial
    for d in range(1, plane):
        pltpu.make_async_remote_copy(
            src_ref=red_src, dst_ref=red_buf.at[d - 1], send_sem=red_sem.at[0],
            recv_sem=red_sem.at[1], device_id=plane_peer(d), device_id_type=MESH,
        ).start()

    for copy in late:
        copy.wait_recv()
    low_image = lower[img]
    use_above = jnp.full((8, LANES), low_image, jnp.int32) == img

    def choose(r, carry):
        for h in range(2):
            for c in range(3):
                partner[RIM + r, h, c] = jnp.where(use_above, above[r, h, c], below[r, h, c])
        return carry

    lax.fori_loop(0, ROWS, choose, 0)
    for half in range(2):
        for side in range(2):
            for c in range(3):
                pack_partner[side, half, c] = packed(
                    lambda r, h: partner[r, h, c], half, side
                )
    partner_rims = send_rims(partner, pack_partner, rim_partner)

    whole = pltpu.make_async_remote_copy(
        src_ref=red_buf, dst_ref=red_buf, send_sem=red_sem.at[0], recv_sem=red_sem.at[1],
        device_id=plane_peer(1), device_id_type=MESH,
    )
    whole.wait_recv()
    line_src[...] = red_src[...] + jnp.sum(red_buf[...], axis=0)
    for d in range(1, n_z):
        pltpu.make_async_remote_copy(
            src_ref=line_src, dst_ref=line_buf.at[d - 1], send_sem=red_sem.at[2],
            recv_sem=red_sem.at[3], device_id=line_peer(d), device_id_type=MESH,
        ).start()

    def assembled(i, k, h, load, load_rim, upper):
        at_a, at_b = h * 64 + k * 8, h * 64 + (7 - k) * 8
        group_a, group_b = (0, 3) if upper else (1, 2)
        a, b = load(i, h), load(EXT - 1 - i, h)
        v = roll_lanes(load_rim(1, group_b), 120 - at_b)
        v = jnp.where(lane < 120, roll_lanes(b, 120), v)
        v = jnp.where(lane < 96, roll_lanes(b, 72), v)
        v = jnp.where(lane < 72, roll_lanes(load_rim(0, group_b), 64 - at_b), v)
        v = jnp.where(lane < 64, roll_lanes(load_rim(1, group_a), 56 - at_a), v)
        v = jnp.where(lane < 56, roll_lanes(a, 56), v)
        v = jnp.where(lane < 32, roll_lanes(a, 8), v)
        return jnp.where(lane < 8, roll_lanes(load_rim(0, group_a), -at_a), v)

    def put_coef(ref, i, h, region):
        aniso = jnp.zeros((8, LANES), jnp.float32)
        damp = jnp.zeros((8, LANES), jnp.float32)
        for n in range(REGIONS):
            inside = region == n
            aniso = jnp.where(inside, anisotropy[n], aniso)
            damp = jnp.where(inside, damping[n], damp)
        ref[i, h, 0] = 2.0 * aniso - 6.0
        ref[i, h, 1] = damp
        ref[i, h, 2] = -TIME_STEP / (1.0 + damp * damp)

    for copy in own_rims + reg_rims:
        copy.wait_recv()

    def main_coefs(r, carry):
        for h in range(2):
            put_coef(main_coef, r, h, reg[r, h])
        return carry

    lax.fori_loop(0, EXT, main_coefs, 0)
    for i in range(ROWS):
        for h in range(2):
            region = assembled(
                i, i % 8, h,
                lambda r, h: reg[r, h].astype(jnp.float32),
                lambda side, g: rim_own[side, g, 3],
                i < 8,
            )
            put_coef(strip_coef, i, h, region.astype(jnp.int32))

    share = jnp.float32(0.0)
    share_all = jnp.float32(0.0)
    for n in range(n_img - 1):
        share = share + jnp.where(n < img, weights[n], 0.0)
        share_all = share_all + weights[n]

    whole_line = pltpu.make_async_remote_copy(
        src_ref=line_buf, dst_ref=line_buf, send_sem=red_sem.at[2], recv_sem=red_sem.at[3],
        device_id=line_peer(1), device_id_type=MESH,
    )
    whole_line.wait_recv()
    squares = line_src[...] + jnp.sum(line_buf[...], axis=0)
    lengths = jnp.where(
        (row_lane >= 1) & (row_lane < n_img), jnp.sqrt(squares + EPS), 0.0
    )
    total = jnp.sum(lengths, axis=1, keepdims=True)
    low_row = jnp.full((1, LANES), low_image, jnp.int32)
    here = jnp.sum(jnp.where(row_lane <= low_row, lengths, 0.0), axis=1, keepdims=True)
    gap = jnp.sum(jnp.where(row_lane == low_row + 1, lengths, 0.0), axis=1, keepdims=True)
    aim = jnp.full((1, 1), share, jnp.float32) / jnp.full((1, 1), share_all, jnp.float32)
    weight = jnp.clip((aim * total - here) / gap, -0.5, 1.5)
    weight = jnp.broadcast_to(weight, (8, LANES))
    own_part = jnp.where(use_above, 1.0 - weight, weight)
    partner_part = jnp.where(use_above, weight, 1.0 - weight)

    def unit(v):
        scale = lax.rsqrt(v[0] * v[0] + v[1] * v[1] + v[2] * v[2])
        return [x * scale for x in v]

    for copy in partner_rims:
        copy.wait_recv()

    def start_main(r, carry):
        for h in range(2):
            v = unit([own_part * own[r, h, c] + partner_part * partner[r, h, c] for c in range(3)])
            for c in range(3):
                main[r, h, c] = v[c]
        return carry

    lax.fori_loop(0, EXT, start_main, 0)
    for side in range(2):
        for g in range(4):
            v = unit([
                own_part * rim_own[side, g, c] + partner_part * rim_partner[side, g, c]
                for c in range(3)
            ])
            for c in range(3):
                rim_start[side, g, c] = v[c]
    for i in range(ROWS):
        for h in range(2):
            for c in range(3):
                strip[i, h, c] = assembled(
                    i, i % 8, h,
                    lambda r, h: main[r, h, c],
                    lambda side, g: rim_start[side, g, c],
                    i < 8,
                )

    def fold(ref):
        for h in range(2):
            for c in range(3):
                ref[ROWS, h, c] = roll_lanes(ref[ROWS - 1, h, c], 64)

    fold(strip)

    first_z, last_z = sub == 0, sub == 7

    def rows_of(fields, i):
        tile, edge = fields
        return [(tile, i), (tile, EXT - 1 - i), (edge, i)]

    def sum_near(fields, i):
        for n, (ref, r) in enumerate(rows_of(fields, i)):
            for h in range(2):
                for c in range(3):
                    v = ref[r, h, c]
                    near[i, n, h, c] = roll_lanes(v, 1) + roll_lanes(v, LANES - 1)

    def moved(ref, coef, r, side_sum):
        rows = ref.at[pl.ds(r - 1, 3)]
        coefs = coef.at[r]
        m = [[rows[1, h, c] for c in range(3)] for h in range(2)]
        moves = []
        for h in range(2):
            lap = []
            for c in range(3):
                here, other = m[h][c], m[1 - h][c]
                if h == 0:
                    edge = jnp.where(first_z, here, pltpu.roll(other, 1, axis=0))
                else:
                    edge = jnp.where(last_z, here, pltpu.roll(other, 7, axis=0))
                beside = rows[0, h, c] + rows[2, h, c]
                lap.append((beside + (other + edge)) + side_sum[h, c])
            mx, my, mz = m[h]
            hx, hy, hz = lap[0] - 6.0 * mx, lap[1] - 6.0 * my, lap[2] + coefs[h, 0] * mz
            damp, scale = coefs[h, 1], coefs[h, 2]
            gx_ = hx + damp * (my * hz - mz * hy)
            gy_ = hy + damp * (mz * hx - mx * hz)
            gz_ = hz + damp * (mx * hy - my * hx)
            moves.append([
                scale * (my * gz_ - mz * gy_),
                scale * (mz * gx_ - mx * gz_),
                scale * (mx * gy_ - my * gx_),
            ])
        return m, moves

    def evaluate(k, source, base, finish):
        coefs = (main_coef, strip_coef)
        sum_near(source, k)

        def step(i, carry):
            sum_near(source, i + 1)
            new = []
            for n, (ref, r) in enumerate(rows_of(source, i)):
                m, moves = moved(ref, coefs[n // 2], r, near.at[i, n])
                old = None if base is None else base[n // 2].at[r]
                for h in range(2):
                    if old is None:
                        v = [m[h][c] + moves[h][c] for c in range(3)]
                    else:
                        v = unit([(old[h, c] + m[h][c]) + moves[h][c] for c in range(3)])
                    new.append(v)
            finish(i, new)
            return carry

        lax.fori_loop(k, ROWS, step, 0)

    def store_to(fields):
        def finish(i, new):
            for n, (ref, r) in enumerate(rows_of(fields, i)):
                for h in range(2):
                    for c in range(3):
                        ref[r, h, c] = new[2 * n + h][c]

        return finish

    def give_out(i, new):
        for n, y in enumerate((i - RIM, EXT - 1 - RIM - i)):
            for h in range(2):
                for c in range(3):
                    s = new[4 + h][c]
                    v = jnp.where(lane < 8, roll_lanes(s, -(64 * n + 8)), new[2 * n + h][c])
                    v = jnp.where(lane >= 120, roll_lanes(s, 72 - 64 * n), v)
                    result[y, h, c] = v
                pltpu.make_async_copy(
                    result.at[y, h], out.at[:, :, h, y, 0, :], out_sem
                ).start()

    now, ahead = (main, strip), (main_next, strip_next)
    for step in range(STEPS):
        k = 2 * step + 1
        evaluate(k, now, None, store_to(ahead))
        fold(strip_next)
        last = step == STEPS - 1
        evaluate(k + 1, ahead, now, give_out if last else store_to(now))
        if not last:
            fold(strip)
    for copy in copies + early + late:
        copy.wait_send()
    whole.wait_send()
    whole_line.wait_send()
    pltpu.make_async_copy(result, result, out_sem).wait()


def body(shape, magnetization, lower_image, image_weights, regions, anisotropy, damping):
    n_img, n_gx, n_gy = shape
    plane = Y_LO * n_gx * n_gy
    f32 = jnp.float32
    tile = (8, LANES)
    smem = pl.BlockSpec(memory_space=pltpu.SMEM)
    anywhere = pl.BlockSpec(memory_space=pl.ANY)
    n_copies = 8 + 2 + 8
    out = pl.pallas_call(
        lambda *refs: kernel(shape, *refs),
        out_shape=jax.ShapeDtypeStruct((3, 8, 2, ROWS, 1, LANES), f32),
        in_specs=[anywhere, anywhere, smem, smem, smem, smem],
        out_specs=anywhere,
        scratch_shapes=[
            pltpu.VMEM((EXT, 2, 3) + tile, f32),
            pltpu.VMEM((ROWS, 2, 3) + tile, f32),
            pltpu.VMEM((ROWS, 2, 3) + tile, f32),
            pltpu.VMEM((EXT, 2, 3) + tile, f32),
            pltpu.VMEM((EXT, 2) + tile, jnp.int32),
            pltpu.VMEM((2, 2, 4) + tile, f32),
            pltpu.VMEM((2, 2, 3) + tile, f32),
            pltpu.VMEM((2, 4, 4) + tile, f32),
            pltpu.VMEM((2, 4, 3) + tile, f32),
            pltpu.VMEM((2, 4, 3) + tile, f32),
            pltpu.VMEM((EXT, 2, 3) + tile, f32),
            pltpu.VMEM((EXT, 2, 3) + tile, f32),
            pltpu.VMEM((EXT, 2, 3) + tile, f32),
            pltpu.VMEM((ROWS + 1, 2, 3) + tile, f32),
            pltpu.VMEM((ROWS + 1, 2, 3) + tile, f32),
            pltpu.VMEM((ROWS, 2, 3) + tile, f32),
            pltpu.VMEM((ROWS + 1, 3, 2, 3) + tile, f32),
            pltpu.VMEM((ROWS, 2, 3) + tile, f32),
            pltpu.VMEM((1, LANES), f32),
            pltpu.VMEM((plane - 1, 1, LANES), f32),
            pltpu.VMEM((1, LANES), f32),
            pltpu.VMEM((n_img // Y_LO - 1, 1, LANES), f32),
            pltpu.SemaphoreType.DMA((2,)),
            pltpu.SemaphoreType.DMA,
            pltpu.SemaphoreType.DMA((2, 4)),
            pltpu.SemaphoreType.DMA((n_copies,)),
            pltpu.SemaphoreType.DMA((n_copies,)),
            pltpu.SemaphoreType.DMA((4,)),
        ],
        compiler_params=pltpu.CompilerParams(collective_id=0, has_side_effects=True),
    )(
        magnetization.reshape(3, 8, 2, ROWS, 1, LANES),
        regions.reshape(8, 2, ROWS, 1, LANES),
        lower_image,
        image_weights,
        anisotropy,
        damping,
    )
    return out.reshape(magnetization.shape)


def solution(mesh):
    placed = (P("img", None, None, "gy", "gx"), P(), P(), P(None, "gy", "gx"), P(), P())
    shape = (mesh.shape["img"], mesh.shape["gx"], mesh.shape["gy"])
    return jax.shard_map(
        lambda *args: body(shape, *args),
        mesh=mesh,
        in_specs=placed,
        out_specs=P("img", None, None, "gy", "gx"),
        check_vma=False,
    )
```

```python
import jax
import jax.numpy as jnp
from jax import lax
from jax.experimental import pallas as pl
from jax.experimental.pallas import tpu as pltpu
from jax.sharding import PartitionSpec as P

STEPS = 4
EPS = 1e-06
TIME_STEP = 0.05
REGIONS = 8

ROWS = 16
RIM = 8
EXT = ROWS + 2 * RIM
HALF = ROWS // 2
LANES = 128
Y_LO = 2
MESH = pl.DeviceIdType.MESH


def roll_lanes(x, shift):
    shift = shift % LANES
    return x if shift == 0 else pltpu.roll(x, shift, axis=1)


def kernel(
    shape,
    mag, regions, lower, weights, anisotropy, damping,
    out,
    own, below, above, partner, reg,
    pack_own, pack_partner, rim_own, rim_partner, rim_start,
    main, main_next, main_coef, strip, strip_next, strip_coef, near, result,
    red_src, red_buf, line_src, line_buf,
    load_sem, out_sem, image_sem, send_sem, recv_sem, red_sem,
):
    n_img, n_gx, n_gy = shape
    n_z = n_img // Y_LO
    img, gx, gy = lax.axis_index("img"), lax.axis_index("gx"), lax.axis_index("gy")
    y_lo, z = img // n_z, img % n_z
    left, right = lax.rem(gx + n_gx - 1, n_gx), lax.rem(gx + 1, n_gx)
    back, front = lax.rem(gy + n_gy - 1, n_gy), lax.rem(gy + 1, n_gy)
    prev, nxt = lax.rem(img + n_img - 1, n_img), lax.rem(img + 1, n_img)

    plane = Y_LO * n_gx * n_gy
    me_plane = (y_lo * n_gx + gx) * n_gy + gy

    def plane_peer(d):
        t = lax.rem(me_plane + d, plane)
        return ((t // (n_gx * n_gy)) * n_z + z, (t // n_gy) % n_gx, t % n_gy)

    def line_peer(d):
        return (y_lo * n_z + lax.rem(z + d, n_z), gx, gy)

    barrier = pltpu.get_barrier_semaphore()
    peers = [(prev, gx, gy), (nxt, gx, gy)]
    peers += [plane_peer(d) for d in range(1, plane)]
    peers += [line_peer(d) for d in range(1, n_z)]
    for peer in peers:
        pl.semaphore_signal(barrier, inc=1, device_id=peer, device_id_type=MESH)

    pl.semaphore_wait(barrier, len(peers))

    to_next, to_prev = (nxt, gx, gy), (prev, gx, gy)

    def send_image(n, rows, field, peer):
        for y in rows:
            for h in range(2):
                pltpu.make_async_remote_copy(
                    src_ref=mag.at[:, :, h, y, 0, :], dst_ref=field.at[y, h],
                    send_sem=image_sem.at[0, n], recv_sem=image_sem.at[1, n],
                    device_id=peer, device_id_type=MESH,
                ).start()
        part = field.at[pl.ds(rows[0], len(rows))]
        return pltpu.make_async_remote_copy(
            src_ref=part, dst_ref=part, send_sem=image_sem.at[0, n],
            recv_sem=image_sem.at[1, n], device_id=peer, device_id_type=MESH,
        )

    low_rows, high_rows = list(range(HALF)), list(range(HALF, ROWS))
    early = [send_image(0, low_rows, below, to_next), send_image(1, high_rows, above, to_prev)]

    for y in range(ROWS):
        for h in range(2):
            pltpu.make_async_copy(
                mag.at[:, :, h, y, 0, :], own.at[RIM + y, h], load_sem.at[0]
            ).start()
    late = [send_image(2, high_rows, below, to_next), send_image(3, low_rows, above, to_prev)]
    for y in range(ROWS):
        for h in range(2):
            pltpu.make_async_copy(
                regions.at[:, h, y, 0, :], reg.at[RIM + y, h], load_sem.at[1]
            ).start()
    inner = pl.ds(RIM, ROWS)
    pltpu.make_async_copy(own.at[inner], own.at[inner], load_sem.at[0]).wait()
    pltpu.make_async_copy(reg.at[inner], reg.at[inner], load_sem.at[1]).wait()

    lane = lax.broadcasted_iota(jnp.int32, (8, LANES), 1)
    sub = lax.broadcasted_iota(jnp.int32, (8, LANES), 0)
    group = lane // RIM

    def packed(load, half, side):
        total = None
        for h in range(2):
            for k in range(8):
                at = h * 64 + k * 8
                piece = roll_lanes(load(RIM + half * 8 + k, h), at + (0 if side == 0 else RIM))
                total = piece if total is None else jnp.where(group == h * 8 + k, piece, total)
        return total

    for half in range(2):
        for side in range(2):
            for c in range(3):
                pack_own[side, half, c] = packed(lambda r, h: own[r, h, c], half, side)
            pack_own[side, half, 3] = packed(
                lambda r, h: reg[r, h].astype(jnp.float32), half, side
            )

    copies = []

    def send(src, dst, peer):
        n = len(copies)
        copy = pltpu.make_async_remote_copy(
            src_ref=src, dst_ref=dst, send_sem=send_sem.at[n], recv_sem=recv_sem.at[n],
            device_id=peer, device_id_type=MESH,
        )
        copy.start()
        copies.append(copy)
        return copy

    def send_rims(field, pack, rim):
        got = [
            send(field.at[pl.ds(RIM, RIM)], field.at[pl.ds(RIM + ROWS, RIM)], (img, gx, back)),
            send(field.at[pl.ds(RIM + HALF, RIM)], field.at[pl.ds(0, RIM)], (img, gx, front)),
            send(pack.at[1], rim.at[0, pl.ds(1, 2)], (img, right, gy)),
            send(pack.at[0], rim.at[1, pl.ds(1, 2)], (img, left, gy)),
            send(pack.at[1, 1], rim.at[0, 0], (img, right, front)),
            send(pack.at[1, 0], rim.at[0, 3], (img, right, back)),
            send(pack.at[0, 1], rim.at[1, 0], (img, left, front)),
            send(pack.at[0, 0], rim.at[1, 3], (img, left, back)),
        ]
        return got

    own_rims = send_rims(own, pack_own, rim_own)
    reg_rims = [
        send(reg.at[pl.ds(RIM, RIM)], reg.at[pl.ds(RIM + ROWS, RIM)], (img, gx, back)),
        send(reg.at[pl.ds(RIM + HALF, RIM)], reg.at[pl.ds(0, RIM)], (img, gx, front)),
    ]

    for copy in early:
        copy.wait_recv()

    def add_squares(r, sums):
        first, second = sums
        for h in range(2):
            for c in range(3):
                d = own[RIM + r, h, c] - below[r, h, c]
                first = first + d * d
                d = own[RIM + HALF + r, h, c] - above[HALF + r, h, c]
                second = second + d * d
        return first, second

    zero = jnp.zeros((8, LANES), jnp.float32)
    first, second = lax.fori_loop(0, HALF, add_squares, (zero, zero))
    row_lane = lax.broadcasted_iota(jnp.int32, (1, LANES), 1)
    partial = jnp.where(row_lane == img, jnp.sum(first), 0.0)
    partial = partial + jnp.where(row_lane == img + 1, jnp.sum(second), 0.0)
    red_src[...] = partial
    for d in range(1, plane):
        pltpu.make_async_remote_copy(
            src_ref=red_src, dst_ref=red_buf.at[d - 1], send_sem=red_sem.at[0],
            recv_sem=red_sem.at[1], device_id=plane_peer(d), device_id_type=MESH,
        ).start()

    for copy in late:
        copy.wait_recv()
    low_image = lower[img]
    use_above = jnp.full((8, LANES), low_image, jnp.int32) == img

    def choose(r, carry):
        for h in range(2):
            for c in range(3):
                partner[RIM + r, h, c] = jnp.where(use_above, above[r, h, c], below[r, h, c])
        return carry

    lax.fori_loop(0, ROWS, choose, 0)
    for half in range(2):
        for side in range(2):
            for c in range(3):
                pack_partner[side, half, c] = packed(
                    lambda r, h: partner[r, h, c], half, side
                )
    partner_rims = send_rims(partner, pack_partner, rim_partner)

    whole = pltpu.make_async_remote_copy(
        src_ref=red_buf, dst_ref=red_buf, send_sem=red_sem.at[0], recv_sem=red_sem.at[1],
        device_id=plane_peer(1), device_id_type=MESH,
    )
    whole.wait_recv()
    line_src[...] = red_src[...] + jnp.sum(red_buf[...], axis=0)
    for d in range(1, n_z):
        pltpu.make_async_remote_copy(
            src_ref=line_src, dst_ref=line_buf.at[d - 1], send_sem=red_sem.at[2],
            recv_sem=red_sem.at[3], device_id=line_peer(d), device_id_type=MESH,
        ).start()

    def assembled(i, k, h, load, load_rim, upper):
        at_a, at_b = h * 64 + k * 8, h * 64 + (7 - k) * 8
        group_a, group_b = (0, 3) if upper else (1, 2)
        a, b = load(i, h), load(EXT - 1 - i, h)
        v = roll_lanes(load_rim(1, group_b), 120 - at_b)
        v = jnp.where(lane < 120, roll_lanes(b, 120), v)
        v = jnp.where(lane < 96, roll_lanes(b, 72), v)
        v = jnp.where(lane < 72, roll_lanes(load_rim(0, group_b), 64 - at_b), v)
        v = jnp.where(lane < 64, roll_lanes(load_rim(1, group_a), 56 - at_a), v)
        v = jnp.where(lane < 56, roll_lanes(a, 56), v)
        v = jnp.where(lane < 32, roll_lanes(a, 8), v)
        return jnp.where(lane < 8, roll_lanes(load_rim(0, group_a), -at_a), v)

    def put_coef(ref, i, h, region):
        aniso = jnp.zeros((8, LANES), jnp.float32)
        damp = jnp.zeros((8, LANES), jnp.float32)
        for n in range(REGIONS):
            inside = region == n
            aniso = jnp.where(inside, anisotropy[n], aniso)
            damp = jnp.where(inside, damping[n], damp)
        ref[i, h, 0] = 2.0 * aniso - 6.0
        ref[i, h, 1] = damp
        ref[i, h, 2] = -TIME_STEP / (1.0 + damp * damp)

    for copy in own_rims + reg_rims:
        copy.wait_recv()

    def main_coefs(r, carry):
        for h in range(2):
            put_coef(main_coef, r, h, reg[r, h])
        return carry

    lax.fori_loop(0, EXT, main_coefs, 0)
    for i in range(ROWS):
        for h in range(2):
            region = assembled(
                i, i % 8, h,
                lambda r, h: reg[r, h].astype(jnp.float32),
                lambda side, g: rim_own[side, g, 3],
                i < 8,
            )
            put_coef(strip_coef, i, h, region.astype(jnp.int32))

    share = jnp.float32(0.0)
    share_all = jnp.float32(0.0)
    for n in range(n_img - 1):
        share = share + jnp.where(n < img, weights[n], 0.0)
        share_all = share_all + weights[n]

    whole_line = pltpu.make_async_remote_copy(
        src_ref=line_buf, dst_ref=line_buf, send_sem=red_sem.at[2], recv_sem=red_sem.at[3],
        device_id=line_peer(1), device_id_type=MESH,
    )
    whole_line.wait_recv()
    squares = line_src[...] + jnp.sum(line_buf[...], axis=0)
    lengths = jnp.where(
        (row_lane >= 1) & (row_lane < n_img), jnp.sqrt(squares + EPS), 0.0
    )
    total = jnp.sum(lengths, axis=1, keepdims=True)
    low_row = jnp.full((1, LANES), low_image, jnp.int32)
    here = jnp.sum(jnp.where(row_lane <= low_row, lengths, 0.0), axis=1, keepdims=True)
    gap = jnp.sum(jnp.where(row_lane == low_row + 1, lengths, 0.0), axis=1, keepdims=True)
    aim = jnp.full((1, 1), share, jnp.float32) / jnp.full((1, 1), share_all, jnp.float32)
    weight = jnp.clip((aim * total - here) / gap, -0.5, 1.5)
    weight = jnp.broadcast_to(weight, (8, LANES))
    own_part = jnp.where(use_above, 1.0 - weight, weight)
    partner_part = jnp.where(use_above, weight, 1.0 - weight)

    def unit(v):
        scale = lax.rsqrt(v[0] * v[0] + v[1] * v[1] + v[2] * v[2])
        return [x * scale for x in v]

    for copy in partner_rims:
        copy.wait_recv()

    def start_main(r, carry):
        for h in range(2):
            v = unit([own_part * own[r, h, c] + partner_part * partner[r, h, c] for c in range(3)])
            for c in range(3):
                main[r, h, c] = v[c]
        return carry

    lax.fori_loop(0, EXT, start_main, 0)
    for side in range(2):
        for g in range(4):
            v = unit([
                own_part * rim_own[side, g, c] + partner_part * rim_partner[side, g, c]
                for c in range(3)
            ])
            for c in range(3):
                rim_start[side, g, c] = v[c]
    for i in range(ROWS):
        for h in range(2):
            for c in range(3):
                strip[i, h, c] = assembled(
                    i, i % 8, h,
                    lambda r, h: main[r, h, c],
                    lambda side, g: rim_start[side, g, c],
                    i < 8,
                )

    def fold(ref):
        for h in range(2):
            for c in range(3):
                ref[ROWS, h, c] = roll_lanes(ref[ROWS - 1, h, c], 64)

    fold(strip)

    first_z, last_z = sub == 0, sub == 7

    def rows_of(fields, i):
        tile, edge = fields
        return [(tile, i), (tile, EXT - 1 - i), (edge, i)]

    def sum_near(fields, i):
        for n, (ref, r) in enumerate(rows_of(fields, i)):
            for h in range(2):
                for c in range(3):
                    v = ref[r, h, c]
                    near[i, n, h, c] = roll_lanes(v, 1) + roll_lanes(v, LANES - 1)

    def moved(ref, coef, r, side_sum):
        rows = ref.at[pl.ds(r - 1, 3)]
        coefs = coef.at[r]
        m = [[rows[1, h, c] for c in range(3)] for h in range(2)]
        moves = []
        for h in range(2):
            lap = []
            for c in range(3):
                here, other = m[h][c], m[1 - h][c]
                if h == 0:
                    edge = jnp.where(first_z, here, pltpu.roll(other, 1, axis=0))
                else:
                    edge = jnp.where(last_z, here, pltpu.roll(other, 7, axis=0))
                beside = rows[0, h, c] + rows[2, h, c]
                lap.append((beside + (other + edge)) + side_sum[h, c])
            mx, my, mz = m[h]
            hx, hy, hz = lap[0] - 6.0 * mx, lap[1] - 6.0 * my, lap[2] + coefs[h, 0] * mz
            damp, scale = coefs[h, 1], coefs[h, 2]
            gx_ = hx + damp * (my * hz - mz * hy)
            gy_ = hy + damp * (mz * hx - mx * hz)
            gz_ = hz + damp * (mx * hy - my * hx)
            moves.append([
                scale * (my * gz_ - mz * gy_),
                scale * (mz * gx_ - mx * gz_),
                scale * (mx * gy_ - my * gx_),
            ])
        return m, moves

    def evaluate(k, source, base, finish):
        coefs = (main_coef, strip_coef)
        sum_near(source, k)
        for i in range(k, ROWS):
            if i + 1 < ROWS:
                sum_near(source, i + 1)
            new = []
            for n, (ref, r) in enumerate(rows_of(source, i)):
                m, moves = moved(ref, coefs[n // 2], r, near.at[i, n])
                old = None if base is None else base[n // 2].at[r]
                for h in range(2):
                    if old is None:
                        v = [m[h][c] + moves[h][c] for c in range(3)]
                    else:
                        v = unit([(old[h, c] + m[h][c]) + moves[h][c] for c in range(3)])
                    new.append(v)
            finish(i, new)

    def store_to(fields):
        def finish(i, new):
            for n, (ref, r) in enumerate(rows_of(fields, i)):
                for h in range(2):
                    for c in range(3):
                        ref[r, h, c] = new[2 * n + h][c]

        return finish

    def give_out(i, new):
        for n, y in enumerate((i - RIM, EXT - 1 - RIM - i)):
            for h in range(2):
                for c in range(3):
                    s = new[4 + h][c]
                    v = jnp.where(lane < 8, roll_lanes(s, -(64 * n + 8)), new[2 * n + h][c])
                    v = jnp.where(lane >= 120, roll_lanes(s, 72 - 64 * n), v)
                    result[y, h, c] = v
                pltpu.make_async_copy(
                    result.at[y, h], out.at[:, :, h, y, 0, :], out_sem
                ).start()

    now, ahead = (main, strip), (main_next, strip_next)
    for step in range(STEPS):
        k = 2 * step + 1
        evaluate(k, now, None, store_to(ahead))
        fold(strip_next)
        last = step == STEPS - 1
        evaluate(k + 1, ahead, now, give_out if last else store_to(now))
        if not last:
            fold(strip)
    for copy in copies + early + late:
        copy.wait_send()
    whole.wait_send()
    whole_line.wait_send()
    pltpu.make_async_copy(result, result, out_sem).wait()


def body(shape, magnetization, lower_image, image_weights, regions, anisotropy, damping):
    n_img, n_gx, n_gy = shape
    plane = Y_LO * n_gx * n_gy
    f32 = jnp.float32
    tile = (8, LANES)
    smem = pl.BlockSpec(memory_space=pltpu.SMEM)
    anywhere = pl.BlockSpec(memory_space=pl.ANY)
    n_copies = 8 + 2 + 8
    out = pl.pallas_call(
        lambda *refs: kernel(shape, *refs),
        out_shape=jax.ShapeDtypeStruct((3, 8, 2, ROWS, 1, LANES), f32),
        in_specs=[anywhere, anywhere, smem, smem, smem, smem],
        out_specs=anywhere,
        scratch_shapes=[
            pltpu.VMEM((EXT, 2, 3) + tile, f32),
            pltpu.VMEM((ROWS, 2, 3) + tile, f32),
            pltpu.VMEM((ROWS, 2, 3) + tile, f32),
            pltpu.VMEM((EXT, 2, 3) + tile, f32),
            pltpu.VMEM((EXT, 2) + tile, jnp.int32),
            pltpu.VMEM((2, 2, 4) + tile, f32),
            pltpu.VMEM((2, 2, 3) + tile, f32),
            pltpu.VMEM((2, 4, 4) + tile, f32),
            pltpu.VMEM((2, 4, 3) + tile, f32),
            pltpu.VMEM((2, 4, 3) + tile, f32),
            pltpu.VMEM((EXT, 2, 3) + tile, f32),
            pltpu.VMEM((EXT, 2, 3) + tile, f32),
            pltpu.VMEM((EXT, 2, 3) + tile, f32),
            pltpu.VMEM((ROWS + 1, 2, 3) + tile, f32),
            pltpu.VMEM((ROWS + 1, 2, 3) + tile, f32),
            pltpu.VMEM((ROWS, 2, 3) + tile, f32),
            pltpu.VMEM((ROWS, 3, 2, 3) + tile, f32),
            pltpu.VMEM((ROWS, 2, 3) + tile, f32),
            pltpu.VMEM((1, LANES), f32),
            pltpu.VMEM((plane - 1, 1, LANES), f32),
            pltpu.VMEM((1, LANES), f32),
            pltpu.VMEM((n_img // Y_LO - 1, 1, LANES), f32),
            pltpu.SemaphoreType.DMA((2,)),
            pltpu.SemaphoreType.DMA,
            pltpu.SemaphoreType.DMA((2, 4)),
            pltpu.SemaphoreType.DMA((n_copies,)),
            pltpu.SemaphoreType.DMA((n_copies,)),
            pltpu.SemaphoreType.DMA((4,)),
        ],
        compiler_params=pltpu.CompilerParams(collective_id=0, has_side_effects=True),
    )(
        magnetization.reshape(3, 8, 2, ROWS, 1, LANES),
        regions.reshape(8, 2, ROWS, 1, LANES),
        lower_image,
        image_weights,
        anisotropy,
        damping,
    )
    return out.reshape(magnetization.shape)


def solution(mesh):
    placed = (P("img", None, None, "gy", "gx"), P(), P(), P(None, "gy", "gx"), P(), P())
    shape = (mesh.shape["img"], mesh.shape["gx"], mesh.shape["gy"])
    return jax.shard_map(
        lambda *args: body(shape, *args),
        mesh=mesh,
        in_specs=placed,
        out_specs=P("img", None, None, "gy", "gx"),
        check_vma=False,
    )
```

```python
import jax
import jax.numpy as jnp
from jax import lax
from jax.experimental import pallas as pl
from jax.experimental.pallas import tpu as pltpu
from jax.sharding import PartitionSpec as P

STEPS = 4
EPS = 1e-06
TIME_STEP = 0.05
REGIONS = 8

ROWS = 16
RIM = 8
EXT = ROWS + 2 * RIM
HALF = ROWS // 2
CHUNKS = 4
LANES = 128
Y_LO = 2
MESH = pl.DeviceIdType.MESH


def roll_lanes(x, shift):
    shift = shift % LANES
    return x if shift == 0 else pltpu.roll(x, shift, axis=1)


def unit(v):
    scale = lax.rsqrt(v[0] * v[0] + v[1] * v[1] + v[2] * v[2])
    return [x * scale for x in v]


def fold(ref):
    for h in range(2):
        for c in range(3):
            ref[ROWS, h, c] = roll_lanes(ref[ROWS - 1, h, c], 64)


def exchange(
    shape,
    mag, regions, lower_in, weights_in, anisotropy_in, damping_in,
    main, main_coef, strip, strip_coef,
    own, below, above, partner, reg,
    pack_own, pack_partner, rim_own, rim_partner,
    own_strip, partner_strip, red_src, red_buf, line_src, line_buf,
    lower, weights, anisotropy, damping, table_sem, load_sem, image_sem, send_sem, recv_sem, red_sem,
):
    n_img, n_gx, n_gy = shape
    n_z = n_img // Y_LO
    img, gx, gy = lax.axis_index("img"), lax.axis_index("gx"), lax.axis_index("gy")
    y_lo, z = img // n_z, img % n_z
    left, right = lax.rem(gx + n_gx - 1, n_gx), lax.rem(gx + 1, n_gx)
    back, front = lax.rem(gy + n_gy - 1, n_gy), lax.rem(gy + 1, n_gy)
    prev, nxt = lax.rem(img + n_img - 1, n_img), lax.rem(img + 1, n_img)

    plane = Y_LO * n_gx * n_gy
    me_plane = (y_lo * n_gx + gx) * n_gy + gy

    def plane_peer(d):
        t = lax.rem(me_plane + d, plane)
        return ((t // (n_gx * n_gy)) * n_z + z, (t // n_gy) % n_gx, t % n_gy)

    def line_peer(d):
        return (y_lo * n_z + lax.rem(z + d, n_z), gx, gy)

    barrier = pltpu.get_barrier_semaphore()
    peers = [(prev, gx, gy), (nxt, gx, gy)]
    peers += [plane_peer(d) for d in range(1, plane)]
    peers += [line_peer(d) for d in range(1, n_z)]
    for peer in peers:
        pl.semaphore_signal(barrier, inc=1, device_id=peer, device_id_type=MESH)

    tables = [
        pltpu.make_async_copy(src, dst, table_sem.at[n])
        for n, (src, dst) in enumerate((
            (lower_in, lower), (weights_in, weights),
            (anisotropy_in, anisotropy), (damping_in, damping),
        ))
    ]
    for copy in tables:
        copy.start()
    pl.semaphore_wait(barrier, len(peers))

    to_next, to_prev = (nxt, gx, gy), (prev, gx, gy)

    def send_images(n, next_rows, prev_rows):
        ways = [(next_rows, below, to_next, n), (prev_rows, above, to_prev, n + 1)]
        for j in range(len(next_rows)):
            for rows, field, peer, m in ways:
                for h in range(2):
                    pltpu.make_async_remote_copy(
                        src_ref=mag.at[:, :, h, rows[j], 0, :], dst_ref=field.at[rows[j], h],
                        send_sem=image_sem.at[0, m], recv_sem=image_sem.at[1, m],
                        device_id=peer, device_id_type=MESH,
                    ).start()
        parts = [(field.at[pl.ds(rows[0], len(rows))], peer, m) for rows, field, peer, m in ways]
        return [
            pltpu.make_async_remote_copy(
                src_ref=part, dst_ref=part, send_sem=image_sem.at[0, m],
                recv_sem=image_sem.at[1, m], device_id=peer, device_id_type=MESH,
            )
            for part, peer, m in parts
        ]

    low_rows, high_rows = list(range(HALF)), list(range(HALF, ROWS))
    early = send_images(0, low_rows, high_rows)

    for y in range(ROWS):
        for h in range(2):
            pltpu.make_async_copy(
                mag.at[:, :, h, y, 0, :], own.at[RIM + y, h], load_sem.at[0]
            ).start()
    step = HALF // CHUNKS
    late = [
        send_images(2 + 2 * q, high_rows[q * step : (q + 1) * step], low_rows[q * step : (q + 1) * step])
        for q in range(CHUNKS)
    ]
    for y in range(ROWS):
        for h in range(2):
            pltpu.make_async_copy(
                regions.at[:, h, y, 0, :], reg.at[RIM + y, h], load_sem.at[1]
            ).start()
    inner = pl.ds(RIM, ROWS)
    pltpu.make_async_copy(own.at[inner], own.at[inner], load_sem.at[0]).wait()
    pltpu.make_async_copy(reg.at[inner], reg.at[inner], load_sem.at[1]).wait()

    lane = lax.broadcasted_iota(jnp.int32, (8, LANES), 1)
    sub = lax.broadcasted_iota(jnp.int32, (8, LANES), 0)
    group = lane // RIM

    def packed(load, half, side):
        total = None
        for h in range(2):
            for k in range(8):
                at = h * 64 + k * 8
                piece = roll_lanes(load(RIM + half * 8 + k, h), at + (0 if side == 0 else RIM))
                total = piece if total is None else jnp.where(group == h * 8 + k, piece, total)
        return total

    for half in range(2):
        for side in range(2):
            for c in range(3):
                pack_own[side, half, c] = packed(lambda r, h: own[r, h, c], half, side)
            pack_own[side, half, 3] = packed(
                lambda r, h: reg[r, h].astype(jnp.float32), half, side
            )

    copies = []

    def send(src, dst, peer):
        n = len(copies)
        copy = pltpu.make_async_remote_copy(
            src_ref=src, dst_ref=dst, send_sem=send_sem.at[n], recv_sem=recv_sem.at[n],
            device_id=peer, device_id_type=MESH,
        )
        copy.start()
        copies.append(copy)
        return copy

    def send_rows(field, first, count):
        return [
            send(
                field.at[pl.ds(RIM + first, count)], field.at[pl.ds(RIM + ROWS + first, count)],
                (img, gx, back),
            ),
            send(
                field.at[pl.ds(RIM + HALF + first, count)], field.at[pl.ds(first, count)],
                (img, gx, front),
            ),
        ]

    def send_packs(pack, rim):
        return [
            send(pack.at[1, 1], rim.at[0, 0], (img, right, front)),
            send(pack.at[1, 0], rim.at[0, 3], (img, right, back)),
            send(pack.at[0, 1], rim.at[1, 0], (img, left, front)),
            send(pack.at[0, 0], rim.at[1, 3], (img, left, back)),
            send(pack.at[1], rim.at[0, pl.ds(1, 2)], (img, right, gy)),
            send(pack.at[0], rim.at[1, pl.ds(1, 2)], (img, left, gy)),
        ]

    own_rims = send_packs(pack_own, rim_own) + send_rows(own, 0, RIM) + send_rows(reg, 0, RIM)

    for copy in early:
        copy.wait_recv()

    def add_squares(r, sums):
        first, second = sums
        for h in range(2):
            for c in range(3):
                d = own[RIM + r, h, c] - below[r, h, c]
                first = first + d * d
                d = own[RIM + HALF + r, h, c] - above[HALF + r, h, c]
                second = second + d * d
        return first, second

    zero = jnp.zeros((8, LANES), jnp.float32)
    first, second = lax.fori_loop(0, HALF, add_squares, (zero, zero))
    row_lane = lax.broadcasted_iota(jnp.int32, (1, LANES), 1)
    partial = jnp.where(row_lane == img, jnp.sum(first), 0.0)
    partial = partial + jnp.where(row_lane == img + 1, jnp.sum(second), 0.0)
    red_src[...] = partial
    for d in range(1, plane):
        pltpu.make_async_remote_copy(
            src_ref=red_src, dst_ref=red_buf.at[d - 1], send_sem=red_sem.at[0],
            recv_sem=red_sem.at[1], device_id=plane_peer(d), device_id_type=MESH,
        ).start()

    for copy in tables:
        copy.wait()
    low_image = lower[img]
    use_above = jnp.full((8, LANES), low_image, jnp.int32) == img
    partner_rims = []
    for q in range(CHUNKS):
        for copy in late[q]:
            copy.wait_recv()
        for r in low_rows[q * step : (q + 1) * step] + high_rows[q * step : (q + 1) * step]:
            for h in range(2):
                for c in range(3):
                    partner[RIM + r, h, c] = jnp.where(use_above, above[r, h, c], below[r, h, c])
        partner_rims += send_rows(partner, q * step, step)
    for half in range(2):
        for side in range(2):
            for c in range(3):
                pack_partner[side, half, c] = packed(
                    lambda r, h: partner[r, h, c], half, side
                )
    partner_rims += send_packs(pack_partner, rim_partner)

    whole = pltpu.make_async_remote_copy(
        src_ref=red_buf, dst_ref=red_buf, send_sem=red_sem.at[0], recv_sem=red_sem.at[1],
        device_id=plane_peer(1), device_id_type=MESH,
    )
    whole.wait_recv()
    line_src[...] = red_src[...] + jnp.sum(red_buf[...], axis=0)
    for d in range(1, n_z):
        pltpu.make_async_remote_copy(
            src_ref=line_src, dst_ref=line_buf.at[d - 1], send_sem=red_sem.at[2],
            recv_sem=red_sem.at[3], device_id=line_peer(d), device_id_type=MESH,
        ).start()

    def assembled(i, k, h, load, load_rim, upper):
        at_a, at_b = h * 64 + k * 8, h * 64 + (7 - k) * 8
        group_a, group_b = (0, 3) if upper else (1, 2)
        a, b = load(i, h), load(EXT - 1 - i, h)
        v = roll_lanes(load_rim(1, group_b), 120 - at_b)
        v = jnp.where(lane < 120, roll_lanes(b, 120), v)
        v = jnp.where(lane < 96, roll_lanes(b, 72), v)
        v = jnp.where(lane < 72, roll_lanes(load_rim(0, group_b), 64 - at_b), v)
        v = jnp.where(lane < 64, roll_lanes(load_rim(1, group_a), 56 - at_a), v)
        v = jnp.where(lane < 56, roll_lanes(a, 56), v)
        v = jnp.where(lane < 32, roll_lanes(a, 8), v)
        return jnp.where(lane < 8, roll_lanes(load_rim(0, group_a), -at_a), v)

    def put_coef(ref, i, h, region):
        aniso = jnp.zeros((8, LANES), jnp.float32)
        damp = jnp.zeros((8, LANES), jnp.float32)
        for n in range(REGIONS):
            inside = region == n
            aniso = jnp.where(inside, anisotropy[n], aniso)
            damp = jnp.where(inside, damping[n], damp)
        ref[i, h, 0] = 2.0 * aniso - 6.0
        ref[i, h, 1] = damp
        ref[i, h, 2] = -TIME_STEP / (1.0 + damp * damp)

    for copy in own_rims:
        copy.wait_recv()

    def main_coefs(r, carry):
        for h in range(2):
            put_coef(main_coef, r, h, reg[r, h])
        return carry

    lax.fori_loop(0, EXT, main_coefs, 0)
    for i in range(ROWS):
        for h in range(2):
            region = assembled(
                i, i % 8, h,
                lambda r, h: reg[r, h].astype(jnp.float32),
                lambda side, g: rim_own[side, g, 3],
                i < 8,
            )
            put_coef(strip_coef, i, h, region.astype(jnp.int32))

    def assemble(into, field, rim):
        for i in range(ROWS):
            for h in range(2):
                for c in range(3):
                    into[i, h, c] = assembled(
                        i, i % 8, h, lambda r, h: field[r, h, c], lambda side, g: rim[side, g, c],
                        i < 8,
                    )

    assemble(own_strip, own, rim_own)

    share = jnp.float32(0.0)
    share_all = jnp.float32(0.0)
    for n in range(n_img - 1):
        share = share + jnp.where(n < img, weights[n], 0.0)
        share_all = share_all + weights[n]

    for copy in partner_rims:
        copy.wait_recv()
    assemble(partner_strip, partner, rim_partner)

    whole_line = pltpu.make_async_remote_copy(
        src_ref=line_buf, dst_ref=line_buf, send_sem=red_sem.at[2], recv_sem=red_sem.at[3],
        device_id=line_peer(1), device_id_type=MESH,
    )
    whole_line.wait_recv()
    squares = line_src[...] + jnp.sum(line_buf[...], axis=0)
    lengths = jnp.where(
        (row_lane >= 1) & (row_lane < n_img), jnp.sqrt(squares + EPS), 0.0
    )
    total = jnp.sum(lengths, axis=1, keepdims=True)
    low_row = jnp.full((1, LANES), low_image, jnp.int32)
    here = jnp.sum(jnp.where(row_lane <= low_row, lengths, 0.0), axis=1, keepdims=True)
    gap = jnp.sum(jnp.where(row_lane == low_row + 1, lengths, 0.0), axis=1, keepdims=True)
    aim = jnp.full((1, 1), share, jnp.float32) / jnp.full((1, 1), share_all, jnp.float32)
    weight = jnp.clip((aim * total - here) / gap, -0.5, 1.5)
    weight = jnp.broadcast_to(weight, (8, LANES))
    own_part = jnp.where(use_above, 1.0 - weight, weight)
    partner_part = jnp.where(use_above, weight, 1.0 - weight)

    def start(into, ours, theirs, count):
        def step(r, carry):
            for h in range(2):
                v = unit([
                    own_part * ours[r, h, c] + partner_part * theirs[r, h, c] for c in range(3)
                ])
                for c in range(3):
                    into[r, h, c] = v[c]
            return carry

        lax.fori_loop(0, count, step, 0, unroll=8)

    start(strip, own_strip, partner_strip, ROWS)
    start(main, own, partner, EXT)
    fold(strip)

    for copy in copies + early + sum(late, []):
        copy.wait_send()
    whole.wait_send()
    whole_line.wait_send()


def evolve(
    main_in, main_coef, strip_in, strip_coef, out,
    main, main_next, strip, strip_next, near, result, out_sem,
):
    lane = lax.broadcasted_iota(jnp.int32, (8, LANES), 1)
    sub = lax.broadcasted_iota(jnp.int32, (8, LANES), 0)
    first_z, last_z = sub == 0, sub == 7

    def rows_of(fields, i):
        tile, edge = fields
        return [(tile, i), (tile, EXT - 1 - i), (edge, i)]

    def sum_near(fields, i):
        for n, (ref, r) in enumerate(rows_of(fields, i)):
            for h in range(2):
                for c in range(3):
                    v = ref[r, h, c]
                    near[i, n, h, c] = roll_lanes(v, 1) + roll_lanes(v, LANES - 1)

    def moved(ref, coef, r, side_sum):
        rows = ref.at[pl.ds(r - 1, 3)]
        coefs = coef.at[r]
        m = [[rows[1, h, c] for c in range(3)] for h in range(2)]
        moves = []
        for h in range(2):
            lap = []
            for c in range(3):
                here, other = m[h][c], m[1 - h][c]
                if h == 0:
                    edge = jnp.where(first_z, here, pltpu.roll(other, 1, axis=0))
                else:
                    edge = jnp.where(last_z, here, pltpu.roll(other, 7, axis=0))
                beside = rows[0, h, c] + rows[2, h, c]
                lap.append((beside + (other + edge)) + side_sum[h, c])
            mx, my, mz = m[h]
            hx, hy, hz = lap[0] - 6.0 * mx, lap[1] - 6.0 * my, lap[2] + coefs[h, 0] * mz
            damp, scale = coefs[h, 1], coefs[h, 2]
            gx_ = hx + damp * (my * hz - mz * hy)
            gy_ = hy + damp * (mz * hx - mx * hz)
            gz_ = hz + damp * (mx * hy - my * hx)
            moves.append([
                scale * (my * gz_ - mz * gy_),
                scale * (mz * gx_ - mx * gz_),
                scale * (mx * gy_ - my * gx_),
            ])
        return m, moves

    def evaluate(k, source, base, finish):
        coefs = (main_coef, strip_coef)
        sum_near(source, k)
        for i in range(k, ROWS):
            if i + 1 < ROWS:
                sum_near(source, i + 1)
            new = []
            for n, (ref, r) in enumerate(rows_of(source, i)):
                m, moves = moved(ref, coefs[n // 2], r, near.at[i, n])
                old = None if base is None else base[n // 2].at[r]
                for h in range(2):
                    if old is None:
                        v = [m[h][c] + moves[h][c] for c in range(3)]
                    else:
                        v = unit([(old[h, c] + m[h][c]) + moves[h][c] for c in range(3)])
                    new.append(v)
            finish(i, new)

    def store_to(fields):
        def finish(i, new):
            for n, (ref, r) in enumerate(rows_of(fields, i)):
                for h in range(2):
                    for c in range(3):
                        ref[r, h, c] = new[2 * n + h][c]

        return finish

    def give_out(i, new):
        for n, y in enumerate((i - RIM, EXT - 1 - RIM - i)):
            for h in range(2):
                for c in range(3):
                    s = new[4 + h][c]
                    v = jnp.where(lane < 8, roll_lanes(s, -(64 * n + 8)), new[2 * n + h][c])
                    v = jnp.where(lane >= 120, roll_lanes(s, 72 - 64 * n), v)
                    result[y, h, c] = v
                pltpu.make_async_copy(
                    result.at[y, h], out.at[:, :, h, y, 0, :], out_sem
                ).start()

    first, now, ahead = (main_in, strip_in), (main, strip), (main_next, strip_next)
    for step in range(STEPS):
        k = 2 * step + 1
        base = now if step else first
        evaluate(k, base, None, store_to(ahead))
        fold(strip_next)
        last = step == STEPS - 1
        evaluate(k + 1, ahead, base, give_out if last else store_to(now))
        if not last:
            fold(strip)
    pltpu.make_async_copy(result, result, out_sem).wait()


def body(shape, magnetization, lower_image, image_weights, regions, anisotropy, damping):
    n_img, n_gx, n_gy = shape
    plane = Y_LO * n_gx * n_gy
    f32 = jnp.float32
    tile = (8, LANES)
    anywhere = pl.BlockSpec(memory_space=pl.ANY)
    n_copies = (6 + 2 + 2) + (6 + 2 * CHUNKS)
    fields = [(EXT, 2, 3) + tile, (EXT, 2, 3) + tile, (ROWS + 1, 2, 3) + tile, (ROWS, 2, 3) + tile]
    vmem = pl.BlockSpec(memory_space=pltpu.VMEM)
    parts = pl.pallas_call(
        lambda *refs: exchange(shape, *refs),
        out_shape=[pltpu.VMEM(dims, f32) for dims in fields],
        in_specs=[anywhere] * 6,
        out_specs=[vmem] * 4,
        scratch_shapes=[
            pltpu.VMEM((EXT, 2, 3) + tile, f32),
            pltpu.VMEM((ROWS, 2, 3) + tile, f32),
            pltpu.VMEM((ROWS, 2, 3) + tile, f32),
            pltpu.VMEM((EXT, 2, 3) + tile, f32),
            pltpu.VMEM((EXT, 2) + tile, jnp.int32),
            pltpu.VMEM((2, 2, 4) + tile, f32),
            pltpu.VMEM((2, 2, 3) + tile, f32),
            pltpu.VMEM((2, 4, 4) + tile, f32),
            pltpu.VMEM((2, 4, 3) + tile, f32),
            pltpu.VMEM((ROWS, 2, 3) + tile, f32),
            pltpu.VMEM((ROWS, 2, 3) + tile, f32),
            pltpu.VMEM((1, LANES), f32),
            pltpu.VMEM((plane - 1, 1, LANES), f32),
            pltpu.VMEM((1, LANES), f32),
            pltpu.VMEM((n_img // Y_LO - 1, 1, LANES), f32),
            pltpu.SMEM((n_img,), jnp.int32),
            pltpu.SMEM((n_img - 1,), f32),
            pltpu.SMEM((REGIONS,), f32),
            pltpu.SMEM((REGIONS,), f32),
            pltpu.SemaphoreType.DMA((4,)),
            pltpu.SemaphoreType.DMA((2,)),
            pltpu.SemaphoreType.DMA((2, 2 + 2 * CHUNKS)),
            pltpu.SemaphoreType.DMA((n_copies,)),
            pltpu.SemaphoreType.DMA((n_copies,)),
            pltpu.SemaphoreType.DMA((4,)),
        ],
        compiler_params=pltpu.CompilerParams(collective_id=0, has_side_effects=True),
    )(
        magnetization.reshape(3, 8, 2, ROWS, 1, LANES),
        regions.reshape(8, 2, ROWS, 1, LANES),
        lower_image,
        image_weights,
        anisotropy,
        damping,
    )
    out = pl.pallas_call(
        evolve,
        out_shape=jax.ShapeDtypeStruct((3, 8, 2, ROWS, 1, LANES), f32),
        in_specs=[vmem] * 4,
        out_specs=anywhere,
        scratch_shapes=[
            pltpu.VMEM((EXT, 2, 3) + tile, f32),
            pltpu.VMEM((EXT, 2, 3) + tile, f32),
            pltpu.VMEM((ROWS + 1, 2, 3) + tile, f32),
            pltpu.VMEM((ROWS + 1, 2, 3) + tile, f32),
            pltpu.VMEM((ROWS, 3, 2, 3) + tile, f32),
            pltpu.VMEM((ROWS, 2, 3) + tile, f32),
            pltpu.SemaphoreType.DMA,
        ],
    )(*[pltpu.with_memory_space_constraint(p, pltpu.VMEM) for p in parts])
    return out.reshape(magnetization.shape)


def solution(mesh):
    placed = (P("img", None, None, "gy", "gx"), P(), P(), P(None, "gy", "gx"), P(), P())
    shape = (mesh.shape["img"], mesh.shape["gx"], mesh.shape["gy"])
    return jax.shard_map(
        lambda *args: body(shape, *args),
        mesh=mesh,
        in_specs=placed,
        out_specs=P("img", None, None, "gy", "gx"),
        check_vma=False,
    )
```

```python
import jax
import jax.numpy as jnp
from jax import lax
from jax.experimental import pallas as pl
from jax.experimental.pallas import tpu as pltpu
from jax.sharding import PartitionSpec as P

STEPS = 4
EPS = 1e-06
TIME_STEP = 0.05
REGIONS = 8

ROWS = 16
RIM = 8
EXT = ROWS + 2 * RIM
HALF = ROWS // 2
CHUNKS = 4
LANES = 128
Y_LO = 2
MESH = pl.DeviceIdType.MESH


def roll_lanes(x, shift):
    shift = shift % LANES
    return x if shift == 0 else pltpu.roll(x, shift, axis=1)


def unit(v):
    scale = lax.rsqrt(v[0] * v[0] + v[1] * v[1] + v[2] * v[2])
    return [x * scale for x in v]


def fold(ref):
    for h in range(2):
        for c in range(3):
            ref[ROWS, h, c] = roll_lanes(ref[ROWS - 1, h, c], 64)


def exchange(
    shape,
    mag, regions, lower_in, weights_in, anisotropy_in, damping_in,
    main, main_coef, strip, strip_coef,
    own, below, above, partner, reg,
    pack_own, pack_partner, rim_own, rim_partner,
    own_strip, partner_strip, red_src, red_buf, line_src, line_buf,
    lower, weights, anisotropy, damping, round_sem, table_sem, load_sem, image_sem, send_sem, recv_sem, red_sem,
):
    n_img, n_gx, n_gy = shape
    n_z = n_img // Y_LO
    img, gx, gy = lax.axis_index("img"), lax.axis_index("gx"), lax.axis_index("gy")
    y_lo, z = img // n_z, img % n_z
    left, right = lax.rem(gx + n_gx - 1, n_gx), lax.rem(gx + 1, n_gx)
    back, front = lax.rem(gy + n_gy - 1, n_gy), lax.rem(gy + 1, n_gy)
    prev, nxt = lax.rem(img + n_img - 1, n_img), lax.rem(img + 1, n_img)

    plane = Y_LO * n_gx * n_gy
    me_plane = (y_lo * n_gx + gx) * n_gy + gy

    def plane_peer(d):
        t = lax.rem(me_plane + d, plane)
        return ((t // (n_gx * n_gy)) * n_z + z, (t // n_gy) % n_gx, t % n_gy)

    def line_peer(d):
        return (y_lo * n_z + lax.rem(z + d, n_z), gx, gy)

    barrier = pltpu.get_barrier_semaphore()
    nearby = [
        (prev, gx, gy), (nxt, gx, gy),
        (img, left, gy), (img, right, gy), (img, gx, back), (img, gx, front),
        (img, left, back), (img, left, front), (img, right, back), (img, right, front),
        (lax.rem(img + n_z, n_img), gx, gy),
    ]

    def tell(sem):
        for peer in nearby:
            pl.semaphore_signal(sem, inc=1, device_id=peer, device_id_type=MESH)

    def heard(sem):
        pl.semaphore_wait(sem, len(nearby))

    tell(barrier)

    tables = [
        pltpu.make_async_copy(src, dst, table_sem.at[n])
        for n, (src, dst) in enumerate((
            (lower_in, lower), (weights_in, weights),
            (anisotropy_in, anisotropy), (damping_in, damping),
        ))
    ]
    for copy in tables:
        copy.start()
    heard(barrier)

    to_next, to_prev = (nxt, gx, gy), (prev, gx, gy)

    def send_images(n, next_rows, prev_rows):
        ways = [(next_rows, below, to_next, n), (prev_rows, above, to_prev, n + 1)]
        for j in range(len(next_rows)):
            for rows, field, peer, m in ways:
                for h in range(2):
                    pltpu.make_async_remote_copy(
                        src_ref=mag.at[:, :, h, rows[j], 0, :], dst_ref=field.at[rows[j], h],
                        send_sem=image_sem.at[0, m], recv_sem=image_sem.at[1, m],
                        device_id=peer, device_id_type=MESH,
                    ).start()
        parts = [(field.at[pl.ds(rows[0], len(rows))], peer, m) for rows, field, peer, m in ways]
        return [
            pltpu.make_async_remote_copy(
                src_ref=part, dst_ref=part, send_sem=image_sem.at[0, m],
                recv_sem=image_sem.at[1, m], device_id=peer, device_id_type=MESH,
            )
            for part, peer, m in parts
        ]

    low_rows, high_rows = list(range(HALF)), list(range(HALF, ROWS))
    tell(round_sem.at[0])
    early = send_images(0, low_rows, high_rows)

    for y in range(ROWS):
        for h in range(2):
            pltpu.make_async_copy(
                mag.at[:, :, h, y, 0, :], own.at[RIM + y, h], load_sem.at[0]
            ).start()
    step = HALF // CHUNKS
    late = [
        send_images(2 + 2 * q, high_rows[q * step : (q + 1) * step], low_rows[q * step : (q + 1) * step])
        for q in range(CHUNKS)
    ]
    for y in range(ROWS):
        for h in range(2):
            pltpu.make_async_copy(
                regions.at[:, h, y, 0, :], reg.at[RIM + y, h], load_sem.at[1]
            ).start()
    inner = pl.ds(RIM, ROWS)
    pltpu.make_async_copy(own.at[inner], own.at[inner], load_sem.at[0]).wait()
    pltpu.make_async_copy(reg.at[inner], reg.at[inner], load_sem.at[1]).wait()

    lane = lax.broadcasted_iota(jnp.int32, (8, LANES), 1)
    sub = lax.broadcasted_iota(jnp.int32, (8, LANES), 0)
    group = lane // RIM

    def packed(load, half, side):
        total = None
        for h in range(2):
            for k in range(8):
                at = h * 64 + k * 8
                piece = roll_lanes(load(RIM + half * 8 + k, h), at + (0 if side == 0 else RIM))
                total = piece if total is None else jnp.where(group == h * 8 + k, piece, total)
        return total

    for half in range(2):
        for side in range(2):
            for c in range(3):
                pack_own[side, half, c] = packed(lambda r, h: own[r, h, c], half, side)
            pack_own[side, half, 3] = packed(
                lambda r, h: reg[r, h].astype(jnp.float32), half, side
            )

    copies = []

    def send(src, dst, peer):
        n = len(copies)
        copy = pltpu.make_async_remote_copy(
            src_ref=src, dst_ref=dst, send_sem=send_sem.at[n], recv_sem=recv_sem.at[n],
            device_id=peer, device_id_type=MESH,
        )
        copy.start()
        copies.append(copy)
        return copy

    def send_rows(field, first, count):
        return [
            send(
                field.at[pl.ds(RIM + first, count)], field.at[pl.ds(RIM + ROWS + first, count)],
                (img, gx, back),
            ),
            send(
                field.at[pl.ds(RIM + HALF + first, count)], field.at[pl.ds(first, count)],
                (img, gx, front),
            ),
        ]

    def send_packs(pack, rim):
        return [
            send(pack.at[1, 1], rim.at[0, 0], (img, right, front)),
            send(pack.at[1, 0], rim.at[0, 3], (img, right, back)),
            send(pack.at[0, 1], rim.at[1, 0], (img, left, front)),
            send(pack.at[0, 0], rim.at[1, 3], (img, left, back)),
            send(pack.at[1], rim.at[0, pl.ds(1, 2)], (img, right, gy)),
            send(pack.at[0], rim.at[1, pl.ds(1, 2)], (img, left, gy)),
        ]

    own_rims = send_packs(pack_own, rim_own) + send_rows(own, 0, RIM) + send_rows(reg, 0, RIM)

    heard(round_sem.at[0])
    tell(round_sem.at[1])

    for copy in early:
        copy.wait_recv()

    def add_squares(r, sums):
        first, second = sums
        for h in range(2):
            for c in range(3):
                d = own[RIM + r, h, c] - below[r, h, c]
                first = first + d * d
                d = own[RIM + HALF + r, h, c] - above[HALF + r, h, c]
                second = second + d * d
        return first, second

    zero = jnp.zeros((8, LANES), jnp.float32)
    first, second = lax.fori_loop(0, HALF, add_squares, (zero, zero))
    heard(round_sem.at[1])
    tell(round_sem.at[2])
    row_lane = lax.broadcasted_iota(jnp.int32, (1, LANES), 1)
    first, second = (
        jnp.sum(jnp.sum(v, axis=0, keepdims=True), axis=1, keepdims=True) for v in (first, second)
    )
    partial = jnp.where(row_lane == img, first, 0.0)
    red_src[...] = partial + jnp.where(row_lane == img + 1, second, 0.0)
    for d in range(1, plane):
        pltpu.make_async_remote_copy(
            src_ref=red_src, dst_ref=red_buf.at[d - 1], send_sem=red_sem.at[0],
            recv_sem=red_sem.at[1], device_id=plane_peer(d), device_id_type=MESH,
        ).start()

    for copy in tables:
        copy.wait()
    low_image = lower[img]
    use_above = jnp.full((8, LANES), low_image, jnp.int32) == img
    partner_rims = []
    for q in range(CHUNKS):
        for copy in late[q]:
            copy.wait_recv()
        for r in low_rows[q * step : (q + 1) * step] + high_rows[q * step : (q + 1) * step]:
            for h in range(2):
                for c in range(3):
                    partner[RIM + r, h, c] = jnp.where(use_above, above[r, h, c], below[r, h, c])
        partner_rims += send_rows(partner, q * step, step)
    for half in range(2):
        for side in range(2):
            for c in range(3):
                pack_partner[side, half, c] = packed(
                    lambda r, h: partner[r, h, c], half, side
                )
    partner_rims += send_packs(pack_partner, rim_partner)

    whole = pltpu.make_async_remote_copy(
        src_ref=red_buf, dst_ref=red_buf, send_sem=red_sem.at[0], recv_sem=red_sem.at[1],
        device_id=plane_peer(1), device_id_type=MESH,
    )
    whole.wait_recv()
    heard(round_sem.at[2])
    line_src[...] = red_src[...] + jnp.sum(red_buf[...], axis=0)
    for d in range(1, n_z):
        pltpu.make_async_remote_copy(
            src_ref=line_src, dst_ref=line_buf.at[d - 1], send_sem=red_sem.at[2],
            recv_sem=red_sem.at[3], device_id=line_peer(d), device_id_type=MESH,
        ).start()

    def assembled(i, k, h, load, load_rim, upper):
        at_a, at_b = h * 64 + k * 8, h * 64 + (7 - k) * 8
        group_a, group_b = (0, 3) if upper else (1, 2)
        a, b = load(i, h), load(EXT - 1 - i, h)
        v = roll_lanes(load_rim(1, group_b), 120 - at_b)
        v = jnp.where(lane < 120, roll_lanes(b, 120), v)
        v = jnp.where(lane < 96, roll_lanes(b, 72), v)
        v = jnp.where(lane < 72, roll_lanes(load_rim(0, group_b), 64 - at_b), v)
        v = jnp.where(lane < 64, roll_lanes(load_rim(1, group_a), 56 - at_a), v)
        v = jnp.where(lane < 56, roll_lanes(a, 56), v)
        v = jnp.where(lane < 32, roll_lanes(a, 8), v)
        return jnp.where(lane < 8, roll_lanes(load_rim(0, group_a), -at_a), v)

    def put_coef(ref, i, h, region):
        aniso = jnp.zeros((8, LANES), jnp.float32)
        damp = jnp.zeros((8, LANES), jnp.float32)
        for n in range(REGIONS):
            inside = region == n
            aniso = jnp.where(inside, anisotropy[n], aniso)
            damp = jnp.where(inside, damping[n], damp)
        ref[i, h, 0] = 2.0 * aniso - 6.0
        ref[i, h, 1] = damp
        ref[i, h, 2] = -TIME_STEP / (1.0 + damp * damp)

    for copy in own_rims:
        copy.wait_recv()

    def main_coefs(r, carry):
        for h in range(2):
            put_coef(main_coef, r, h, reg[r, h])
        return carry

    lax.fori_loop(0, EXT, main_coefs, 0)
    for i in range(ROWS):
        for h in range(2):
            region = assembled(
                i, i % 8, h,
                lambda r, h: reg[r, h].astype(jnp.float32),
                lambda side, g: rim_own[side, g, 3],
                i < 8,
            )
            put_coef(strip_coef, i, h, region.astype(jnp.int32))

    def assemble(into, field, rim):
        for i in range(ROWS):
            for h in range(2):
                for c in range(3):
                    into[i, h, c] = assembled(
                        i, i % 8, h, lambda r, h: field[r, h, c], lambda side, g: rim[side, g, c],
                        i < 8,
                    )

    assemble(own_strip, own, rim_own)

    share = jnp.float32(0.0)
    share_all = jnp.float32(0.0)
    for n in range(n_img - 1):
        share = share + jnp.where(n < img, weights[n], 0.0)
        share_all = share_all + weights[n]

    for copy in partner_rims:
        copy.wait_recv()
    assemble(partner_strip, partner, rim_partner)

    whole_line = pltpu.make_async_remote_copy(
        src_ref=line_buf, dst_ref=line_buf, send_sem=red_sem.at[2], recv_sem=red_sem.at[3],
        device_id=line_peer(1), device_id_type=MESH,
    )
    whole_line.wait_recv()
    squares = line_src[...] + jnp.sum(line_buf[...], axis=0)
    lengths = jnp.where(
        (row_lane >= 1) & (row_lane < n_img), jnp.sqrt(squares + EPS), 0.0
    )
    total = jnp.sum(lengths, axis=1, keepdims=True)
    low_row = jnp.full((1, LANES), low_image, jnp.int32)
    here = jnp.sum(jnp.where(row_lane <= low_row, lengths, 0.0), axis=1, keepdims=True)
    gap = jnp.sum(jnp.where(row_lane == low_row + 1, lengths, 0.0), axis=1, keepdims=True)
    aim = jnp.full((1, 1), share, jnp.float32) / jnp.full((1, 1), share_all, jnp.float32)
    weight = jnp.clip((aim * total - here) / gap, -0.5, 1.5)
    weight = jnp.broadcast_to(weight, (8, LANES))
    own_part = jnp.where(use_above, 1.0 - weight, weight)
    partner_part = jnp.where(use_above, weight, 1.0 - weight)

    def start(into, ours, theirs, count):
        def step(r, carry):
            for h in range(2):
                v = unit([
                    own_part * ours[r, h, c] + partner_part * theirs[r, h, c] for c in range(3)
                ])
                for c in range(3):
                    into[r, h, c] = v[c]
            return carry

        lax.fori_loop(0, count, step, 0, unroll=8)

    start(strip, own_strip, partner_strip, ROWS)
    start(main, own, partner, EXT)
    fold(strip)

    for copy in copies + early + sum(late, []):
        copy.wait_send()
    whole.wait_send()
    whole_line.wait_send()


def evolve(
    main_in, main_coef, strip_in, strip_coef, out,
    main, main_next, strip, strip_next, near, result, out_sem,
):
    lane = lax.broadcasted_iota(jnp.int32, (8, LANES), 1)
    sub = lax.broadcasted_iota(jnp.int32, (8, LANES), 0)
    first_z, last_z = sub == 0, sub == 7

    def rows_of(fields, i):
        tile, edge = fields
        return [(tile, i), (tile, EXT - 1 - i), (edge, i)]

    def sum_near(fields, i):
        for n, (ref, r) in enumerate(rows_of(fields, i)):
            for h in range(2):
                for c in range(3):
                    v = ref[r, h, c]
                    near[i, n, h, c] = roll_lanes(v, 1) + roll_lanes(v, LANES - 1)

    def moved(ref, coef, r, side_sum):
        rows = ref.at[pl.ds(r - 1, 3)]
        coefs = coef.at[r]
        m = [[rows[1, h, c] for c in range(3)] for h in range(2)]
        moves = []
        for h in range(2):
            lap = []
            for c in range(3):
                here, other = m[h][c], m[1 - h][c]
                if h == 0:
                    edge = jnp.where(first_z, here, pltpu.roll(other, 1, axis=0))
                else:
                    edge = jnp.where(last_z, here, pltpu.roll(other, 7, axis=0))
                beside = rows[0, h, c] + rows[2, h, c]
                lap.append((beside + (other + edge)) + side_sum[h, c])
            mx, my, mz = m[h]
            hx, hy, hz = lap[0] - 6.0 * mx, lap[1] - 6.0 * my, lap[2] + coefs[h, 0] * mz
            damp, scale = coefs[h, 1], coefs[h, 2]
            gx_ = hx + damp * (my * hz - mz * hy)
            gy_ = hy + damp * (mz * hx - mx * hz)
            gz_ = hz + damp * (mx * hy - my * hx)
            moves.append([
                scale * (my * gz_ - mz * gy_),
                scale * (mz * gx_ - mx * gz_),
                scale * (mx * gy_ - my * gx_),
            ])
        return m, moves

    def evaluate(k, source, base, finish):
        coefs = (main_coef, strip_coef)
        sum_near(source, k)
        for i in range(k, ROWS):
            if i + 1 < ROWS:
                sum_near(source, i + 1)
            new = []
            for n, (ref, r) in enumerate(rows_of(source, i)):
                m, moves = moved(ref, coefs[n // 2], r, near.at[i, n])
                old = None if base is None else base[n // 2].at[r]
                for h in range(2):
                    if old is None:
                        v = [m[h][c] + moves[h][c] for c in range(3)]
                    else:
                        v = unit([(old[h, c] + m[h][c]) + moves[h][c] for c in range(3)])
                    new.append(v)
            finish(i, new)

    def store_to(fields):
        def finish(i, new):
            for n, (ref, r) in enumerate(rows_of(fields, i)):
                for h in range(2):
                    for c in range(3):
                        ref[r, h, c] = new[2 * n + h][c]

        return finish

    def give_out(i, new):
        for n, y in enumerate((i - RIM, EXT - 1 - RIM - i)):
            for h in range(2):
                for c in range(3):
                    s = new[4 + h][c]
                    v = jnp.where(lane < 8, roll_lanes(s, -(64 * n + 8)), new[2 * n + h][c])
                    v = jnp.where(lane >= 120, roll_lanes(s, 72 - 64 * n), v)
                    result[y, h, c] = v
                pltpu.make_async_copy(
                    result.at[y, h], out.at[:, :, h, y, 0, :], out_sem
                ).start()

    first, now, ahead = (main_in, strip_in), (main, strip), (main_next, strip_next)
    for step in range(STEPS):
        k = 2 * step + 1
        base = now if step else first
        evaluate(k, base, None, store_to(ahead))
        fold(strip_next)
        last = step == STEPS - 1
        evaluate(k + 1, ahead, base, give_out if last else store_to(now))
        if not last:
            fold(strip)
    pltpu.make_async_copy(result, result, out_sem).wait()


def body(shape, magnetization, lower_image, image_weights, regions, anisotropy, damping):
    n_img, n_gx, n_gy = shape
    plane = Y_LO * n_gx * n_gy
    f32 = jnp.float32
    tile = (8, LANES)
    anywhere = pl.BlockSpec(memory_space=pl.ANY)
    n_copies = (6 + 2 + 2) + (6 + 2 * CHUNKS)
    fields = [(EXT, 2, 3) + tile, (EXT, 2, 3) + tile, (ROWS + 1, 2, 3) + tile, (ROWS, 2, 3) + tile]
    vmem = pl.BlockSpec(memory_space=pltpu.VMEM)
    parts = pl.pallas_call(
        lambda *refs: exchange(shape, *refs),
        out_shape=[pltpu.VMEM(dims, f32) for dims in fields],
        in_specs=[anywhere] * 6,
        out_specs=[vmem] * 4,
        scratch_shapes=[
            pltpu.VMEM((EXT, 2, 3) + tile, f32),
            pltpu.VMEM((ROWS, 2, 3) + tile, f32),
            pltpu.VMEM((ROWS, 2, 3) + tile, f32),
            pltpu.VMEM((EXT, 2, 3) + tile, f32),
            pltpu.VMEM((EXT, 2) + tile, jnp.int32),
            pltpu.VMEM((2, 2, 4) + tile, f32),
            pltpu.VMEM((2, 2, 3) + tile, f32),
            pltpu.VMEM((2, 4, 4) + tile, f32),
            pltpu.VMEM((2, 4, 3) + tile, f32),
            pltpu.VMEM((ROWS, 2, 3) + tile, f32),
            pltpu.VMEM((ROWS, 2, 3) + tile, f32),
            pltpu.VMEM((1, LANES), f32),
            pltpu.VMEM((plane - 1, 1, LANES), f32),
            pltpu.VMEM((1, LANES), f32),
            pltpu.VMEM((n_img // Y_LO - 1, 1, LANES), f32),
            pltpu.SMEM((n_img,), jnp.int32),
            pltpu.SMEM((n_img - 1,), f32),
            pltpu.SMEM((REGIONS,), f32),
            pltpu.SMEM((REGIONS,), f32),
            pltpu.SemaphoreType.REGULAR((3,)),
            pltpu.SemaphoreType.DMA((4,)),
            pltpu.SemaphoreType.DMA((2,)),
            pltpu.SemaphoreType.DMA((2, 2 + 2 * CHUNKS)),
            pltpu.SemaphoreType.DMA((n_copies,)),
            pltpu.SemaphoreType.DMA((n_copies,)),
            pltpu.SemaphoreType.DMA((4,)),
        ],
        compiler_params=pltpu.CompilerParams(collective_id=0, has_side_effects=True),
    )(
        magnetization.reshape(3, 8, 2, ROWS, 1, LANES),
        regions.reshape(8, 2, ROWS, 1, LANES),
        lower_image,
        image_weights,
        anisotropy,
        damping,
    )
    out = pl.pallas_call(
        evolve,
        out_shape=jax.ShapeDtypeStruct((3, 8, 2, ROWS, 1, LANES), f32),
        in_specs=[vmem] * 4,
        out_specs=anywhere,
        scratch_shapes=[
            pltpu.VMEM((EXT, 2, 3) + tile, f32),
            pltpu.VMEM((EXT, 2, 3) + tile, f32),
            pltpu.VMEM((ROWS + 1, 2, 3) + tile, f32),
            pltpu.VMEM((ROWS + 1, 2, 3) + tile, f32),
            pltpu.VMEM((ROWS, 3, 2, 3) + tile, f32),
            pltpu.VMEM((ROWS, 2, 3) + tile, f32),
            pltpu.SemaphoreType.DMA,
        ],
    )(*[pltpu.with_memory_space_constraint(p, pltpu.VMEM) for p in parts])
    return out.reshape(magnetization.shape)


def solution(mesh):
    placed = (P("img", None, None, "gy", "gx"), P(), P(), P(None, "gy", "gx"), P(), P())
    shape = (mesh.shape["img"], mesh.shape["gx"], mesh.shape["gy"])
    return jax.shard_map(
        lambda *args: body(shape, *args),
        mesh=mesh,
        in_specs=placed,
        out_specs=P("img", None, None, "gy", "gx"),
        check_vma=False,
    )
```

```python
import jax
import jax.numpy as jnp
from jax import lax
from jax.experimental import pallas as pl
from jax.experimental.pallas import tpu as pltpu
from jax.sharding import PartitionSpec as P

STEPS = 4
EPS = 1e-06
TIME_STEP = 0.05
REGIONS = 8

ROWS = 16
RIM = 8
EXT = ROWS + 2 * RIM
HALF = ROWS // 2
CHUNKS = 4
LANES = 128
Y_LO = 2
MESH = pl.DeviceIdType.MESH


def roll_lanes(x, shift):
    shift = shift % LANES
    return x if shift == 0 else pltpu.roll(x, shift, axis=1)


def unit(v):
    scale = lax.rsqrt(v[0] * v[0] + v[1] * v[1] + v[2] * v[2])
    return [x * scale for x in v]


def fold(ref):
    for h in range(2):
        for c in range(3):
            ref[ROWS, h, c] = roll_lanes(ref[ROWS - 1, h, c], 64)


def exchange(
    shape,
    mag, regions, lower_in, weights_in, anisotropy_in, damping_in,
    main, main_coef, strip, strip_coef,
    own, below, above, partner, reg,
    pack_own, pack_partner, rim_own, rim_partner,
    own_strip, partner_strip, red_src, red_buf, line_src, line_buf,
    lower, weights, anisotropy, damping, round_sem, table_sem, load_sem, image_sem, send_sem, recv_sem, red_sem,
):
    n_img, n_gx, n_gy = shape
    n_z = n_img // Y_LO
    img, gx, gy = lax.axis_index("img"), lax.axis_index("gx"), lax.axis_index("gy")
    y_lo, z = img // n_z, img % n_z
    left, right = lax.rem(gx + n_gx - 1, n_gx), lax.rem(gx + 1, n_gx)
    back, front = lax.rem(gy + n_gy - 1, n_gy), lax.rem(gy + 1, n_gy)
    prev, nxt = lax.rem(img + n_img - 1, n_img), lax.rem(img + 1, n_img)

    plane = Y_LO * n_gx * n_gy
    me_plane = (y_lo * n_gx + gx) * n_gy + gy

    def plane_peer(d):
        t = lax.rem(me_plane + d, plane)
        return ((t // (n_gx * n_gy)) * n_z + z, (t // n_gy) % n_gx, t % n_gy)

    def line_peer(d):
        return (y_lo * n_z + lax.rem(z + d, n_z), gx, gy)

    barrier = pltpu.get_barrier_semaphore()
    nearby = [
        (prev, gx, gy), (nxt, gx, gy),
        (img, left, gy), (img, right, gy), (img, gx, back), (img, gx, front),
        (img, left, back), (img, left, front), (img, right, back), (img, right, front),
        (lax.rem(img + n_z, n_img), gx, gy),
    ]

    def tell(sem):
        for peer in nearby:
            pl.semaphore_signal(sem, inc=1, device_id=peer, device_id_type=MESH)

    def heard(sem):
        pl.semaphore_wait(sem, len(nearby))

    tell(barrier)

    tables = [
        pltpu.make_async_copy(src, dst, table_sem.at[n])
        for n, (src, dst) in enumerate((
            (lower_in, lower), (weights_in, weights),
            (anisotropy_in, anisotropy), (damping_in, damping),
        ))
    ]
    for copy in tables:
        copy.start()
    heard(barrier)

    to_next, to_prev = (nxt, gx, gy), (prev, gx, gy)

    def send_images(n, next_rows, prev_rows):
        ways = [(next_rows, below, to_next, n), (prev_rows, above, to_prev, n + 1)]
        for j in range(len(next_rows)):
            for rows, field, peer, m in ways:
                for h in range(2):
                    pltpu.make_async_remote_copy(
                        src_ref=mag.at[:, :, h, rows[j], 0, :], dst_ref=field.at[rows[j], h],
                        send_sem=image_sem.at[0, m], recv_sem=image_sem.at[1, m],
                        device_id=peer, device_id_type=MESH,
                    ).start()
        parts = [(field.at[pl.ds(rows[0], len(rows))], peer, m) for rows, field, peer, m in ways]
        return [
            pltpu.make_async_remote_copy(
                src_ref=part, dst_ref=part, send_sem=image_sem.at[0, m],
                recv_sem=image_sem.at[1, m], device_id=peer, device_id_type=MESH,
            )
            for part, peer, m in parts
        ]

    low_rows, high_rows = list(range(HALF)), list(range(HALF, ROWS))
    tell(round_sem.at[0])
    early = send_images(0, low_rows, high_rows)

    for y in range(ROWS):
        for h in range(2):
            pltpu.make_async_copy(
                mag.at[:, :, h, y, 0, :], own.at[RIM + y, h], load_sem.at[0]
            ).start()
    step = HALF // CHUNKS
    late = [
        send_images(2 + 2 * q, high_rows[q * step : (q + 1) * step], low_rows[q * step : (q + 1) * step])
        for q in range(CHUNKS)
    ]
    for y in range(ROWS):
        for h in range(2):
            pltpu.make_async_copy(
                regions.at[:, h, y, 0, :], reg.at[RIM + y, h], load_sem.at[1]
            ).start()
    inner = pl.ds(RIM, ROWS)

    lane = lax.broadcasted_iota(jnp.int32, (8, LANES), 1)
    sub = lax.broadcasted_iota(jnp.int32, (8, LANES), 0)
    group = lane // RIM

    def add_to_pack(pack, c, load, first, count):
        for half in range(2):
            for side in range(2):
                total = pack[side, half, c] if first else None
                for h in range(2):
                    for k in range(first, first + count):
                        at = h * 64 + k * 8 + (0 if side == 0 else RIM)
                        piece = roll_lanes(load(RIM + half * 8 + k, h), at)
                        if total is None:
                            total = piece
                        else:
                            total = jnp.where(group == h * 8 + k, piece, total)
                pack[side, half, c] = total

    copies = []

    def send(src, dst, peer):
        n = len(copies)
        copy = pltpu.make_async_remote_copy(
            src_ref=src, dst_ref=dst, send_sem=send_sem.at[n], recv_sem=recv_sem.at[n],
            device_id=peer, device_id_type=MESH,
        )
        copy.start()
        copies.append(copy)
        return copy

    def send_rows(field, first, count):
        return [
            send(
                field.at[pl.ds(RIM + first, count)], field.at[pl.ds(RIM + ROWS + first, count)],
                (img, gx, back),
            ),
            send(
                field.at[pl.ds(RIM + HALF + first, count)], field.at[pl.ds(first, count)],
                (img, gx, front),
            ),
        ]

    def send_packs(pack, rim):
        return [
            send(pack.at[1, 1], rim.at[0, 0], (img, right, front)),
            send(pack.at[1, 0], rim.at[0, 3], (img, right, back)),
            send(pack.at[0, 1], rim.at[1, 0], (img, left, front)),
            send(pack.at[0, 0], rim.at[1, 3], (img, left, back)),
            send(pack.at[1], rim.at[0, pl.ds(1, 2)], (img, right, gy)),
            send(pack.at[0], rim.at[1, pl.ds(1, 2)], (img, left, gy)),
        ]

    pltpu.make_async_copy(own.at[inner], own.at[inner], load_sem.at[0]).wait()
    own_rims = send_rows(own, 0, RIM)
    pltpu.make_async_copy(reg.at[inner], reg.at[inner], load_sem.at[1]).wait()
    own_rims += send_rows(reg, 0, RIM)
    for c in range(3):
        add_to_pack(pack_own, c, lambda r, h: own[r, h, c], 0, 8)
    add_to_pack(pack_own, 3, lambda r, h: reg[r, h].astype(jnp.float32), 0, 8)
    own_rims += send_packs(pack_own, rim_own)

    heard(round_sem.at[0])
    tell(round_sem.at[1])

    for copy in early:
        copy.wait_recv()

    def add_squares(r, sums):
        first, second = sums
        for h in range(2):
            for c in range(3):
                d = own[RIM + r, h, c] - below[r, h, c]
                first = first + d * d
                d = own[RIM + HALF + r, h, c] - above[HALF + r, h, c]
                second = second + d * d
        return first, second

    zero = jnp.zeros((8, LANES), jnp.float32)
    first, second = lax.fori_loop(0, HALF, add_squares, (zero, zero))
    heard(round_sem.at[1])
    tell(round_sem.at[2])
    row_lane = lax.broadcasted_iota(jnp.int32, (1, LANES), 1)
    first, second = (
        jnp.sum(jnp.sum(v, axis=0, keepdims=True), axis=1, keepdims=True) for v in (first, second)
    )
    partial = jnp.where(row_lane == img, first, 0.0)
    red_src[...] = partial + jnp.where(row_lane == img + 1, second, 0.0)
    for d in range(1, plane):
        pltpu.make_async_remote_copy(
            src_ref=red_src, dst_ref=red_buf.at[d - 1], send_sem=red_sem.at[0],
            recv_sem=red_sem.at[1], device_id=plane_peer(d), device_id_type=MESH,
        ).start()

    for copy in tables:
        copy.wait()
    low_image = lower[img]
    use_above = jnp.full((8, LANES), low_image, jnp.int32) == img
    partner_rows = []
    for q in range(CHUNKS):
        for copy in late[q]:
            copy.wait_recv()
        for r in low_rows[q * step : (q + 1) * step] + high_rows[q * step : (q + 1) * step]:
            for h in range(2):
                for c in range(3):
                    partner[RIM + r, h, c] = jnp.where(use_above, above[r, h, c], below[r, h, c])
        if q < CHUNKS - 1:
            partner_rows += send_rows(partner, q * step, step)
        for c in range(3):
            add_to_pack(pack_partner, c, lambda r, h: partner[r, h, c], q * step, step)
    partner_packs = send_packs(pack_partner, rim_partner)
    partner_rows += send_rows(partner, HALF - step, step)

    whole = pltpu.make_async_remote_copy(
        src_ref=red_buf, dst_ref=red_buf, send_sem=red_sem.at[0], recv_sem=red_sem.at[1],
        device_id=plane_peer(1), device_id_type=MESH,
    )
    whole.wait_recv()
    heard(round_sem.at[2])
    line_src[...] = red_src[...] + jnp.sum(red_buf[...], axis=0)
    for d in range(1, n_z):
        pltpu.make_async_remote_copy(
            src_ref=line_src, dst_ref=line_buf.at[d - 1], send_sem=red_sem.at[2],
            recv_sem=red_sem.at[3], device_id=line_peer(d), device_id_type=MESH,
        ).start()

    def inner_part(i, h, load):
        a, b = load(i, h), load(EXT - 1 - i, h)
        v = jnp.where(lane < 96, roll_lanes(b, 72), roll_lanes(b, 120))
        v = jnp.where(lane < 64, roll_lanes(a, 56), v)
        return jnp.where(lane < 32, roll_lanes(a, 8), v)

    def with_rims(v, i, h, load_rim):
        at_a, at_b = h * 64 + (i % 8) * 8, h * 64 + (7 - i % 8) * 8
        group_a, group_b = (0, 3) if i < 8 else (1, 2)
        v = jnp.where(group == 0, roll_lanes(load_rim(0, group_a), -at_a), v)
        v = jnp.where(group == 7, roll_lanes(load_rim(1, group_a), 56 - at_a), v)
        v = jnp.where(group == 8, roll_lanes(load_rim(0, group_b), 64 - at_b), v)
        return jnp.where(group == 15, roll_lanes(load_rim(1, group_b), 120 - at_b), v)

    def put_coef(ref, i, h, region):
        aniso = jnp.zeros((8, LANES), jnp.float32)
        damp = jnp.zeros((8, LANES), jnp.float32)
        for n in range(REGIONS):
            inside = region == n
            aniso = jnp.where(inside, anisotropy[n], aniso)
            damp = jnp.where(inside, damping[n], damp)
        ref[i, h, 0] = 2.0 * aniso - 6.0
        ref[i, h, 1] = damp
        ref[i, h, 2] = -TIME_STEP / (1.0 + damp * damp)

    for copy in own_rims:
        copy.wait_recv()

    def main_coefs(r, carry):
        for h in range(2):
            put_coef(main_coef, r, h, reg[r, h])
        return carry

    lax.fori_loop(0, EXT, main_coefs, 0)
    for i in range(ROWS):
        for h in range(2):
            region = with_rims(
                inner_part(i, h, lambda r, h: reg[r, h].astype(jnp.float32)),
                i, h, lambda side, g: rim_own[side, g, 3],
            )
            put_coef(strip_coef, i, h, region.astype(jnp.int32))

    for i in range(ROWS):
        for h in range(2):
            for c in range(3):
                own_strip[i, h, c] = with_rims(
                    inner_part(i, h, lambda r, h: own[r, h, c]),
                    i, h, lambda side, g: rim_own[side, g, c],
                )

    share = jnp.float32(0.0)
    share_all = jnp.float32(0.0)
    for n in range(n_img - 1):
        share = share + jnp.where(n < img, weights[n], 0.0)
        share_all = share_all + weights[n]

    whole_line = pltpu.make_async_remote_copy(
        src_ref=line_buf, dst_ref=line_buf, send_sem=red_sem.at[2], recv_sem=red_sem.at[3],
        device_id=line_peer(1), device_id_type=MESH,
    )
    whole_line.wait_recv()
    squares = line_src[...] + jnp.sum(line_buf[...], axis=0)
    lengths = jnp.where(
        (row_lane >= 1) & (row_lane < n_img), jnp.sqrt(squares + EPS), 0.0
    )
    total = jnp.sum(lengths, axis=1, keepdims=True)
    low_row = jnp.full((1, LANES), low_image, jnp.int32)
    here = jnp.sum(jnp.where(row_lane <= low_row, lengths, 0.0), axis=1, keepdims=True)
    gap = jnp.sum(jnp.where(row_lane == low_row + 1, lengths, 0.0), axis=1, keepdims=True)
    aim = jnp.full((1, 1), share, jnp.float32) / jnp.full((1, 1), share_all, jnp.float32)
    weight = jnp.clip((aim * total - here) / gap, -0.5, 1.5)
    weight = jnp.broadcast_to(weight, (8, LANES))
    own_part = jnp.where(use_above, 1.0 - weight, weight)
    partner_part = jnp.where(use_above, weight, 1.0 - weight)

    def mixed(ours, theirs):
        return unit([own_part * a + partner_part * b for a, b in zip(ours, theirs)])

    for copy in partner_rows:
        copy.wait_recv()

    def start_row(r, carry):
        for h in range(2):
            v = mixed([own[r, h, c] for c in range(3)], [partner[r, h, c] for c in range(3)])
            for c in range(3):
                main[r, h, c] = v[c]
        return carry

    lax.fori_loop(0, EXT, start_row, 0, unroll=8)
    for i in range(ROWS):
        for h in range(2):
            for c in range(3):
                partner_strip[i, h, c] = inner_part(i, h, lambda r, h: partner[r, h, c])
    for copy in partner_packs:
        copy.wait_recv()
    for i in range(ROWS):
        for h in range(2):
            v = mixed(
                [own_strip[i, h, c] for c in range(3)],
                [
                    with_rims(
                        partner_strip[i, h, c], i, h, lambda side, g: rim_partner[side, g, c]
                    )
                    for c in range(3)
                ],
            )
            for c in range(3):
                strip[i, h, c] = v[c]
    fold(strip)

    for copy in copies + early + sum(late, []):
        copy.wait_send()
    whole.wait_send()
    whole_line.wait_send()


def evolve(
    main_in, main_coef, strip_in, strip_coef, out,
    main, main_next, strip, strip_next, near, result, out_sem,
):
    lane = lax.broadcasted_iota(jnp.int32, (8, LANES), 1)
    sub = lax.broadcasted_iota(jnp.int32, (8, LANES), 0)
    first_z, last_z = sub == 0, sub == 7

    def rows_of(fields, i):
        tile, edge = fields
        return [(tile, i), (tile, EXT - 1 - i), (edge, i)]

    def sum_near(fields, i):
        for n, (ref, r) in enumerate(rows_of(fields, i)):
            for h in range(2):
                for c in range(3):
                    v = ref[r, h, c]
                    near[i, n, h, c] = roll_lanes(v, 1) + roll_lanes(v, LANES - 1)

    def moved(ref, coef, r, side_sum):
        rows = ref.at[pl.ds(r - 1, 3)]
        coefs = coef.at[r]
        m = [[rows[1, h, c] for c in range(3)] for h in range(2)]
        moves = []
        for h in range(2):
            lap = []
            for c in range(3):
                here, other = m[h][c], m[1 - h][c]
                if h == 0:
                    edge = jnp.where(first_z, here, pltpu.roll(other, 1, axis=0))
                else:
                    edge = jnp.where(last_z, here, pltpu.roll(other, 7, axis=0))
                beside = rows[0, h, c] + rows[2, h, c]
                lap.append((beside + (other + edge)) + side_sum[h, c])
            mx, my, mz = m[h]
            hx, hy, hz = lap[0] - 6.0 * mx, lap[1] - 6.0 * my, lap[2] + coefs[h, 0] * mz
            damp, scale = coefs[h, 1], coefs[h, 2]
            gx_ = hx + damp * (my * hz - mz * hy)
            gy_ = hy + damp * (mz * hx - mx * hz)
            gz_ = hz + damp * (mx * hy - my * hx)
            moves.append([
                scale * (my * gz_ - mz * gy_),
                scale * (mz * gx_ - mx * gz_),
                scale * (mx * gy_ - my * gx_),
            ])
        return m, moves

    def evaluate(k, source, base, finish):
        coefs = (main_coef, strip_coef)
        sum_near(source, k)
        for i in range(k, ROWS):
            if i + 1 < ROWS:
                sum_near(source, i + 1)
            new = []
            for n, (ref, r) in enumerate(rows_of(source, i)):
                m, moves = moved(ref, coefs[n // 2], r, near.at[i, n])
                old = None if base is None else base[n // 2].at[r]
                for h in range(2):
                    if old is None:
                        v = [m[h][c] + moves[h][c] for c in range(3)]
                    else:
                        v = unit([(old[h, c] + m[h][c]) + moves[h][c] for c in range(3)])
                    new.append(v)
            finish(i, new)

    def store_to(fields):
        def finish(i, new):
            for n, (ref, r) in enumerate(rows_of(fields, i)):
                for h in range(2):
                    for c in range(3):
                        ref[r, h, c] = new[2 * n + h][c]

        return finish

    def give_out(i, new):
        for n, y in enumerate((i - RIM, EXT - 1 - RIM - i)):
            for h in range(2):
                for c in range(3):
                    s = new[4 + h][c]
                    v = jnp.where(lane < 8, roll_lanes(s, -(64 * n + 8)), new[2 * n + h][c])
                    v = jnp.where(lane >= 120, roll_lanes(s, 72 - 64 * n), v)
                    result[y, h, c] = v
                pltpu.make_async_copy(
                    result.at[y, h], out.at[:, :, h, y, 0, :], out_sem
                ).start()

    first, now, ahead = (main_in, strip_in), (main, strip), (main_next, strip_next)
    for step in range(STEPS):
        k = 2 * step + 1
        base = now if step else first
        evaluate(k, base, None, store_to(ahead))
        fold(strip_next)
        last = step == STEPS - 1
        evaluate(k + 1, ahead, base, give_out if last else store_to(now))
        if not last:
            fold(strip)
    pltpu.make_async_copy(result, result, out_sem).wait()


def body(shape, magnetization, lower_image, image_weights, regions, anisotropy, damping):
    n_img, n_gx, n_gy = shape
    plane = Y_LO * n_gx * n_gy
    f32 = jnp.float32
    tile = (8, LANES)
    anywhere = pl.BlockSpec(memory_space=pl.ANY)
    n_copies = (6 + 2 + 2) + (6 + 2 * CHUNKS)
    fields = [(EXT, 2, 3) + tile, (EXT, 2, 3) + tile, (ROWS + 1, 2, 3) + tile, (ROWS, 2, 3) + tile]
    vmem = pl.BlockSpec(memory_space=pltpu.VMEM)
    parts = pl.pallas_call(
        lambda *refs: exchange(shape, *refs),
        out_shape=[pltpu.VMEM(dims, f32) for dims in fields],
        in_specs=[anywhere] * 6,
        out_specs=[vmem] * 4,
        scratch_shapes=[
            pltpu.VMEM((EXT, 2, 3) + tile, f32),
            pltpu.VMEM((ROWS, 2, 3) + tile, f32),
            pltpu.VMEM((ROWS, 2, 3) + tile, f32),
            pltpu.VMEM((EXT, 2, 3) + tile, f32),
            pltpu.VMEM((EXT, 2) + tile, jnp.int32),
            pltpu.VMEM((2, 2, 4) + tile, f32),
            pltpu.VMEM((2, 2, 3) + tile, f32),
            pltpu.VMEM((2, 4, 4) + tile, f32),
            pltpu.VMEM((2, 4, 3) + tile, f32),
            pltpu.VMEM((ROWS, 2, 3) + tile, f32),
            pltpu.VMEM((ROWS, 2, 3) + tile, f32),
            pltpu.VMEM((1, LANES), f32),
            pltpu.VMEM((plane - 1, 1, LANES), f32),
            pltpu.VMEM((1, LANES), f32),
            pltpu.VMEM((n_img // Y_LO - 1, 1, LANES), f32),
            pltpu.SMEM((n_img,), jnp.int32),
            pltpu.SMEM((n_img - 1,), f32),
            pltpu.SMEM((REGIONS,), f32),
            pltpu.SMEM((REGIONS,), f32),
            pltpu.SemaphoreType.REGULAR((3,)),
            pltpu.SemaphoreType.DMA((4,)),
            pltpu.SemaphoreType.DMA((2,)),
            pltpu.SemaphoreType.DMA((2, 2 + 2 * CHUNKS)),
            pltpu.SemaphoreType.DMA((n_copies,)),
            pltpu.SemaphoreType.DMA((n_copies,)),
            pltpu.SemaphoreType.DMA((4,)),
        ],
        compiler_params=pltpu.CompilerParams(collective_id=0, has_side_effects=True),
    )(
        magnetization.reshape(3, 8, 2, ROWS, 1, LANES),
        regions.reshape(8, 2, ROWS, 1, LANES),
        lower_image,
        image_weights,
        anisotropy,
        damping,
    )
    out = pl.pallas_call(
        evolve,
        out_shape=jax.ShapeDtypeStruct((3, 8, 2, ROWS, 1, LANES), f32),
        in_specs=[vmem] * 4,
        out_specs=anywhere,
        scratch_shapes=[
            pltpu.VMEM((EXT, 2, 3) + tile, f32),
            pltpu.VMEM((EXT, 2, 3) + tile, f32),
            pltpu.VMEM((ROWS + 1, 2, 3) + tile, f32),
            pltpu.VMEM((ROWS + 1, 2, 3) + tile, f32),
            pltpu.VMEM((ROWS, 3, 2, 3) + tile, f32),
            pltpu.VMEM((ROWS, 2, 3) + tile, f32),
            pltpu.SemaphoreType.DMA,
        ],
    )(*[pltpu.with_memory_space_constraint(p, pltpu.VMEM) for p in parts])
    return out.reshape(magnetization.shape)


def solution(mesh):
    placed = (P("img", None, None, "gy", "gx"), P(), P(), P(None, "gy", "gx"), P(), P())
    shape = (mesh.shape["img"], mesh.shape["gx"], mesh.shape["gy"])
    return jax.shard_map(
        lambda *args: body(shape, *args),
        mesh=mesh,
        in_specs=placed,
        out_specs=P("img", None, None, "gy", "gx"),
        check_vma=False,
    )
```

```python
import jax
import jax.numpy as jnp
from jax import lax
from jax.experimental import pallas as pl
from jax.experimental.pallas import tpu as pltpu
from jax.sharding import PartitionSpec as P

STEPS = 4
EPS = 1e-06
TIME_STEP = 0.05
REGIONS = 8

ROWS = 16
RIM = 8
EXT = ROWS + 2 * RIM
HALF = ROWS // 2
CHUNKS = 4
LANES = 128
Y_LO = 2
MESH = pl.DeviceIdType.MESH


def roll_lanes(x, shift):
    shift = shift % LANES
    return x if shift == 0 else pltpu.roll(x, shift, axis=1)


def unit(v):
    scale = lax.rsqrt(v[0] * v[0] + v[1] * v[1] + v[2] * v[2])
    return [x * scale for x in v]


def fold(ref):
    for h in range(2):
        for c in range(3):
            ref[ROWS, h, c] = roll_lanes(ref[ROWS - 1, h, c], 64)


def exchange(
    shape,
    mag, regions, lower_in, weights_in, anisotropy_in, damping_in,
    main, main_coef, strip, strip_coef,
    own, below, above, partner, reg,
    pack_own, pack_partner, rim_own, rim_partner,
    own_strip, partner_strip, red_src, red_buf, line_src, line_buf,
    lower, weights, anisotropy, damping, round_sem, table_sem, load_sem, image_sem, send_sem, recv_sem, red_sem,
):
    n_img, n_gx, n_gy = shape
    n_z = n_img // Y_LO
    img, gx, gy = lax.axis_index("img"), lax.axis_index("gx"), lax.axis_index("gy")
    y_lo, z = img // n_z, img % n_z
    left, right = lax.rem(gx + n_gx - 1, n_gx), lax.rem(gx + 1, n_gx)
    back, front = lax.rem(gy + n_gy - 1, n_gy), lax.rem(gy + 1, n_gy)
    prev, nxt = lax.rem(img + n_img - 1, n_img), lax.rem(img + 1, n_img)

    plane = Y_LO * n_gx * n_gy

    def plane_peer(d):
        a, b, c = d // (n_gx * n_gy), (d // n_gy) % n_gx, d % n_gy
        there = lax.rem(y_lo + a, Y_LO) * n_z + z
        return (there, lax.rem(gx + b, n_gx), lax.rem(gy + c, n_gy))

    def line_peer(d):
        return (y_lo * n_z + lax.rem(z + d, n_z), gx, gy)

    barrier = pltpu.get_barrier_semaphore()
    nearby = [
        (prev, gx, gy), (nxt, gx, gy),
        (img, left, gy), (img, right, gy), (img, gx, back), (img, gx, front),
        (img, left, back), (img, left, front), (img, right, back), (img, right, front),
        (lax.rem(img + n_z, n_img), gx, gy),
    ]

    def tell(sem):
        for peer in nearby:
            pl.semaphore_signal(sem, inc=1, device_id=peer, device_id_type=MESH)

    def heard(sem):
        pl.semaphore_wait(sem, len(nearby))

    tell(barrier)

    tables = [
        pltpu.make_async_copy(src, dst, table_sem.at[n])
        for n, (src, dst) in enumerate((
            (lower_in, lower), (weights_in, weights),
            (anisotropy_in, anisotropy), (damping_in, damping),
        ))
    ]
    for copy in tables:
        copy.start()
    heard(barrier)

    to_next, to_prev = (nxt, gx, gy), (prev, gx, gy)

    def send_images(n, next_rows, prev_rows):
        ways = [(next_rows, below, to_next, n), (prev_rows, above, to_prev, n + 1)]
        for j in range(len(next_rows)):
            for rows, field, peer, m in ways:
                for h in range(2):
                    pltpu.make_async_remote_copy(
                        src_ref=mag.at[:, :, h, rows[j], 0, :], dst_ref=field.at[rows[j], h],
                        send_sem=image_sem.at[0, m], recv_sem=image_sem.at[1, m],
                        device_id=peer, device_id_type=MESH,
                    ).start()
        parts = [(field.at[pl.ds(rows[0], len(rows))], peer, m) for rows, field, peer, m in ways]
        return [
            pltpu.make_async_remote_copy(
                src_ref=part, dst_ref=part, send_sem=image_sem.at[0, m],
                recv_sem=image_sem.at[1, m], device_id=peer, device_id_type=MESH,
            )
            for part, peer, m in parts
        ]

    low_rows, high_rows = list(range(HALF)), list(range(HALF, ROWS))
    tell(round_sem.at[0])
    early = send_images(0, low_rows, high_rows)

    for y in range(ROWS):
        for h in range(2):
            pltpu.make_async_copy(
                mag.at[:, :, h, y, 0, :], own.at[RIM + y, h], load_sem.at[0]
            ).start()
    step = HALF // CHUNKS
    late = [
        send_images(2 + 2 * q, high_rows[q * step : (q + 1) * step], low_rows[q * step : (q + 1) * step])
        for q in range(CHUNKS)
    ]
    for y in range(ROWS):
        for h in range(2):
            pltpu.make_async_copy(
                regions.at[:, h, y, 0, :], reg.at[RIM + y, h], load_sem.at[1]
            ).start()
    inner = pl.ds(RIM, ROWS)

    lane = lax.broadcasted_iota(jnp.int32, (8, LANES), 1)
    sub = lax.broadcasted_iota(jnp.int32, (8, LANES), 0)
    group = lane // RIM

    def add_to_pack(pack, c, load, first, count):
        for half in range(2):
            for side in range(2):
                total = pack[side, half, c] if first else None
                for h in range(2):
                    for k in range(first, first + count):
                        at = h * 64 + k * 8 + (0 if side == 0 else RIM)
                        piece = roll_lanes(load(RIM + half * 8 + k, h), at)
                        if total is None:
                            total = piece
                        else:
                            total = jnp.where(group == h * 8 + k, piece, total)
                pack[side, half, c] = total

    copies = []

    def send(src, dst, peer):
        n = len(copies)
        copy = pltpu.make_async_remote_copy(
            src_ref=src, dst_ref=dst, send_sem=send_sem.at[n], recv_sem=recv_sem.at[n],
            device_id=peer, device_id_type=MESH,
        )
        copy.start()
        copies.append(copy)
        return copy

    def send_rows(field, first, count):
        return [
            send(
                field.at[pl.ds(RIM + first, count)], field.at[pl.ds(RIM + ROWS + first, count)],
                (img, gx, back),
            ),
            send(
                field.at[pl.ds(RIM + HALF + first, count)], field.at[pl.ds(first, count)],
                (img, gx, front),
            ),
        ]

    def send_packs(pack, rim):
        return [
            send(pack.at[1, 1], rim.at[0, 0], (img, right, front)),
            send(pack.at[1, 0], rim.at[0, 3], (img, right, back)),
            send(pack.at[0, 1], rim.at[1, 0], (img, left, front)),
            send(pack.at[0, 0], rim.at[1, 3], (img, left, back)),
            send(pack.at[1], rim.at[0, pl.ds(1, 2)], (img, right, gy)),
            send(pack.at[0], rim.at[1, pl.ds(1, 2)], (img, left, gy)),
        ]

    pltpu.make_async_copy(own.at[inner], own.at[inner], load_sem.at[0]).wait()
    own_rims = send_rows(own, 0, RIM)
    pltpu.make_async_copy(reg.at[inner], reg.at[inner], load_sem.at[1]).wait()
    own_rims += send_rows(reg, 0, RIM)
    for c in range(3):
        add_to_pack(pack_own, c, lambda r, h: own[r, h, c], 0, 8)
    add_to_pack(pack_own, 3, lambda r, h: reg[r, h].astype(jnp.float32), 0, 8)
    own_rims += send_packs(pack_own, rim_own)

    heard(round_sem.at[0])
    tell(round_sem.at[1])

    for copy in early:
        copy.wait_recv()

    def add_squares(r, sums):
        first, second = sums
        for h in range(2):
            for c in range(3):
                d = own[RIM + r, h, c] - below[r, h, c]
                first = first + d * d
                d = own[RIM + HALF + r, h, c] - above[HALF + r, h, c]
                second = second + d * d
        return first, second

    zero = jnp.zeros((8, LANES), jnp.float32)
    first, second = lax.fori_loop(0, HALF, add_squares, (zero, zero), unroll=4)
    heard(round_sem.at[1])
    row_lane = lax.broadcasted_iota(jnp.int32, (1, LANES), 1)
    first, second = (
        jnp.sum(jnp.sum(v, axis=0, keepdims=True), axis=1, keepdims=True) for v in (first, second)
    )
    partial = jnp.where(row_lane == img, first, 0.0)
    red_src[...] = partial + jnp.where(row_lane == img + 1, second, 0.0)
    for d in sorted(range(1, plane), key=lambda d: -min(d % n_gy, n_gy - d % n_gy)):
        pltpu.make_async_remote_copy(
            src_ref=red_src, dst_ref=red_buf.at[d - 1], send_sem=red_sem.at[0],
            recv_sem=red_sem.at[1], device_id=plane_peer(d), device_id_type=MESH,
        ).start()

    tell(round_sem.at[2])

    for copy in tables:
        copy.wait()
    low_image = lower[img]
    use_above = jnp.full((8, LANES), low_image, jnp.int32) == img
    partner_rows = []
    for q in range(CHUNKS):
        for copy in late[q]:
            copy.wait_recv()
        for r in low_rows[q * step : (q + 1) * step] + high_rows[q * step : (q + 1) * step]:
            for h in range(2):
                for c in range(3):
                    partner[RIM + r, h, c] = jnp.where(use_above, above[r, h, c], below[r, h, c])
        if q < CHUNKS - 1:
            partner_rows += send_rows(partner, q * step, step)
        for c in range(3):
            add_to_pack(pack_partner, c, lambda r, h: partner[r, h, c], q * step, step)
    partner_packs = send_packs(pack_partner, rim_partner)
    partner_rows += send_rows(partner, HALF - step, step)

    whole = pltpu.make_async_remote_copy(
        src_ref=red_buf, dst_ref=red_buf, send_sem=red_sem.at[0], recv_sem=red_sem.at[1],
        device_id=plane_peer(1), device_id_type=MESH,
    )
    whole.wait_recv()
    heard(round_sem.at[2])
    line_src[...] = red_src[...] + jnp.sum(red_buf[...], axis=0)
    for d in sorted(range(1, n_z), key=lambda d: -min(d, n_z - d)):
        pltpu.make_async_remote_copy(
            src_ref=line_src, dst_ref=line_buf.at[d - 1], send_sem=red_sem.at[2],
            recv_sem=red_sem.at[3], device_id=line_peer(d), device_id_type=MESH,
        ).start()

    def inner_part(i, h, load):
        a, b = load(i, h), load(EXT - 1 - i, h)
        v = jnp.where(lane < 96, roll_lanes(b, 72), roll_lanes(b, 120))
        v = jnp.where(lane < 64, roll_lanes(a, 56), v)
        return jnp.where(lane < 32, roll_lanes(a, 8), v)

    def with_rims(v, i, h, load_rim):
        at_a, at_b = h * 64 + (i % 8) * 8, h * 64 + (7 - i % 8) * 8
        group_a, group_b = (0, 3) if i < 8 else (1, 2)
        v = jnp.where(group == 0, roll_lanes(load_rim(0, group_a), -at_a), v)
        v = jnp.where(group == 7, roll_lanes(load_rim(1, group_a), 56 - at_a), v)
        v = jnp.where(group == 8, roll_lanes(load_rim(0, group_b), 64 - at_b), v)
        return jnp.where(group == 15, roll_lanes(load_rim(1, group_b), 120 - at_b), v)

    def put_coef(ref, i, h, region):
        aniso = jnp.zeros((8, LANES), jnp.float32)
        damp = jnp.zeros((8, LANES), jnp.float32)
        for n in range(REGIONS):
            inside = region == n
            aniso = jnp.where(inside, anisotropy[n], aniso)
            damp = jnp.where(inside, damping[n], damp)
        ref[i, h, 0] = 2.0 * aniso - 6.0
        ref[i, h, 1] = damp
        ref[i, h, 2] = -TIME_STEP / (1.0 + damp * damp)

    for copy in own_rims:
        copy.wait_recv()

    def main_coefs(r, carry):
        for h in range(2):
            put_coef(main_coef, r, h, reg[r, h])
        return carry

    lax.fori_loop(0, EXT, main_coefs, 0)
    for i in range(ROWS):
        for h in range(2):
            region = with_rims(
                inner_part(i, h, lambda r, h: reg[r, h].astype(jnp.float32)),
                i, h, lambda side, g: rim_own[side, g, 3],
            )
            put_coef(strip_coef, i, h, region.astype(jnp.int32))

    for i in range(ROWS):
        for h in range(2):
            for c in range(3):
                own_strip[i, h, c] = with_rims(
                    inner_part(i, h, lambda r, h: own[r, h, c]),
                    i, h, lambda side, g: rim_own[side, g, c],
                )

    share = jnp.float32(0.0)
    share_all = jnp.float32(0.0)
    for n in range(n_img - 1):
        share = share + jnp.where(n < img, weights[n], 0.0)
        share_all = share_all + weights[n]

    whole_line = pltpu.make_async_remote_copy(
        src_ref=line_buf, dst_ref=line_buf, send_sem=red_sem.at[2], recv_sem=red_sem.at[3],
        device_id=line_peer(1), device_id_type=MESH,
    )
    whole_line.wait_recv()
    squares = line_src[...] + jnp.sum(line_buf[...], axis=0)
    lengths = jnp.where(
        (row_lane >= 1) & (row_lane < n_img), jnp.sqrt(squares + EPS), 0.0
    )
    total = jnp.sum(lengths, axis=1, keepdims=True)
    low_row = jnp.full((1, LANES), low_image, jnp.int32)
    here = jnp.sum(jnp.where(row_lane <= low_row, lengths, 0.0), axis=1, keepdims=True)
    gap = jnp.sum(jnp.where(row_lane == low_row + 1, lengths, 0.0), axis=1, keepdims=True)
    aim = jnp.full((1, 1), share, jnp.float32) / jnp.full((1, 1), share_all, jnp.float32)
    weight = jnp.clip((aim * total - here) / gap, -0.5, 1.5)
    weight = jnp.broadcast_to(weight, (8, LANES))
    own_part = jnp.where(use_above, 1.0 - weight, weight)
    partner_part = jnp.where(use_above, weight, 1.0 - weight)

    def mixed(ours, theirs):
        return unit([own_part * a + partner_part * b for a, b in zip(ours, theirs)])

    for copy in partner_rows:
        copy.wait_recv()

    def start_row(r, carry):
        for h in range(2):
            v = mixed([own[r, h, c] for c in range(3)], [partner[r, h, c] for c in range(3)])
            for c in range(3):
                main[r, h, c] = v[c]
        return carry

    lax.fori_loop(0, EXT, start_row, 0, unroll=8)
    for i in range(ROWS):
        for h in range(2):
            for c in range(3):
                partner_strip[i, h, c] = inner_part(i, h, lambda r, h: partner[r, h, c])
    for copy in partner_packs:
        copy.wait_recv()
    for i in range(ROWS):
        for h in range(2):
            v = mixed(
                [own_strip[i, h, c] for c in range(3)],
                [
                    with_rims(
                        partner_strip[i, h, c], i, h, lambda side, g: rim_partner[side, g, c]
                    )
                    for c in range(3)
                ],
            )
            for c in range(3):
                strip[i, h, c] = v[c]
    fold(strip)

    for copy in copies + early + sum(late, []):
        copy.wait_send()
    whole.wait_send()
    whole_line.wait_send()


def evolve(
    main_in, main_coef, strip_in, strip_coef, out,
    main, main_next, strip, strip_next, near, result, out_sem,
):
    lane = lax.broadcasted_iota(jnp.int32, (8, LANES), 1)
    sub = lax.broadcasted_iota(jnp.int32, (8, LANES), 0)
    first_z, last_z = sub == 0, sub == 7

    def rows_of(fields, i):
        tile, edge = fields
        return [(tile, i), (tile, EXT - 1 - i), (edge, i)]

    def sum_near(fields, i):
        for n, (ref, r) in enumerate(rows_of(fields, i)):
            for h in range(2):
                for c in range(3):
                    v = ref[r, h, c]
                    near[i, n, h, c] = roll_lanes(v, 1) + roll_lanes(v, LANES - 1)

    def moved(ref, coef, r, side_sum):
        rows = ref.at[pl.ds(r - 1, 3)]
        coefs = coef.at[r]
        m = [[rows[1, h, c] for c in range(3)] for h in range(2)]
        moves = []
        for h in range(2):
            lap = []
            for c in range(3):
                here, other = m[h][c], m[1 - h][c]
                if h == 0:
                    edge = jnp.where(first_z, here, pltpu.roll(other, 1, axis=0))
                else:
                    edge = jnp.where(last_z, here, pltpu.roll(other, 7, axis=0))
                beside = rows[0, h, c] + rows[2, h, c]
                lap.append((beside + (other + edge)) + side_sum[h, c])
            mx, my, mz = m[h]
            hx, hy, hz = lap[0] - 6.0 * mx, lap[1] - 6.0 * my, lap[2] + coefs[h, 0] * mz
            damp, scale = coefs[h, 1], coefs[h, 2]
            gx_ = hx + damp * (my * hz - mz * hy)
            gy_ = hy + damp * (mz * hx - mx * hz)
            gz_ = hz + damp * (mx * hy - my * hx)
            moves.append([
                scale * (my * gz_ - mz * gy_),
                scale * (mz * gx_ - mx * gz_),
                scale * (mx * gy_ - my * gx_),
            ])
        return m, moves

    def evaluate(k, source, base, finish):
        coefs = (main_coef, strip_coef)
        sum_near(source, k)
        for i in range(k, ROWS):
            if i + 1 < ROWS:
                sum_near(source, i + 1)
            new = []
            for n, (ref, r) in enumerate(rows_of(source, i)):
                m, moves = moved(ref, coefs[n // 2], r, near.at[i, n])
                old = None if base is None else base[n // 2].at[r]
                for h in range(2):
                    if old is None:
                        v = [m[h][c] + moves[h][c] for c in range(3)]
                    else:
                        v = unit([(old[h, c] + m[h][c]) + moves[h][c] for c in range(3)])
                    new.append(v)
            finish(i, new)

    def store_to(fields):
        def finish(i, new):
            for n, (ref, r) in enumerate(rows_of(fields, i)):
                for h in range(2):
                    for c in range(3):
                        ref[r, h, c] = new[2 * n + h][c]

        return finish

    def give_out(i, new):
        for n, y in enumerate((i - RIM, EXT - 1 - RIM - i)):
            for h in range(2):
                for c in range(3):
                    s = new[4 + h][c]
                    v = jnp.where(lane < 8, roll_lanes(s, -(64 * n + 8)), new[2 * n + h][c])
                    v = jnp.where(lane >= 120, roll_lanes(s, 72 - 64 * n), v)
                    result[y, h, c] = v
                pltpu.make_async_copy(
                    result.at[y, h], out.at[:, :, h, y, 0, :], out_sem
                ).start()

    first, now, ahead = (main_in, strip_in), (main, strip), (main_next, strip_next)
    for step in range(STEPS):
        k = 2 * step + 1
        base = now if step else first
        evaluate(k, base, None, store_to(ahead))
        fold(strip_next)
        last = step == STEPS - 1
        evaluate(k + 1, ahead, base, give_out if last else store_to(now))
        if not last:
            fold(strip)
    pltpu.make_async_copy(result, result, out_sem).wait()


def body(shape, magnetization, lower_image, image_weights, regions, anisotropy, damping):
    n_img, n_gx, n_gy = shape
    plane = Y_LO * n_gx * n_gy
    f32 = jnp.float32
    tile = (8, LANES)
    anywhere = pl.BlockSpec(memory_space=pl.ANY)
    n_copies = (6 + 2 + 2) + (6 + 2 * CHUNKS)
    fields = [(EXT, 2, 3) + tile, (EXT, 2, 3) + tile, (ROWS + 1, 2, 3) + tile, (ROWS, 2, 3) + tile]
    vmem = pl.BlockSpec(memory_space=pltpu.VMEM)
    parts = pl.pallas_call(
        lambda *refs: exchange(shape, *refs),
        out_shape=[pltpu.VMEM(dims, f32) for dims in fields],
        in_specs=[anywhere] * 6,
        out_specs=[vmem] * 4,
        scratch_shapes=[
            pltpu.VMEM((EXT, 2, 3) + tile, f32),
            pltpu.VMEM((ROWS, 2, 3) + tile, f32),
            pltpu.VMEM((ROWS, 2, 3) + tile, f32),
            pltpu.VMEM((EXT, 2, 3) + tile, f32),
            pltpu.VMEM((EXT, 2) + tile, jnp.int32),
            pltpu.VMEM((2, 2, 4) + tile, f32),
            pltpu.VMEM((2, 2, 3) + tile, f32),
            pltpu.VMEM((2, 4, 4) + tile, f32),
            pltpu.VMEM((2, 4, 3) + tile, f32),
            pltpu.VMEM((ROWS, 2, 3) + tile, f32),
            pltpu.VMEM((ROWS, 2, 3) + tile, f32),
            pltpu.VMEM((1, LANES), f32),
            pltpu.VMEM((plane - 1, 1, LANES), f32),
            pltpu.VMEM((1, LANES), f32),
            pltpu.VMEM((n_img // Y_LO - 1, 1, LANES), f32),
            pltpu.SMEM((n_img,), jnp.int32),
            pltpu.SMEM((n_img - 1,), f32),
            pltpu.SMEM((REGIONS,), f32),
            pltpu.SMEM((REGIONS,), f32),
            pltpu.SemaphoreType.REGULAR((3,)),
            pltpu.SemaphoreType.DMA((4,)),
            pltpu.SemaphoreType.DMA((2,)),
            pltpu.SemaphoreType.DMA((2, 2 + 2 * CHUNKS)),
            pltpu.SemaphoreType.DMA((n_copies,)),
            pltpu.SemaphoreType.DMA((n_copies,)),
            pltpu.SemaphoreType.DMA((4,)),
        ],
        compiler_params=pltpu.CompilerParams(collective_id=0, has_side_effects=True),
    )(
        magnetization.reshape(3, 8, 2, ROWS, 1, LANES),
        regions.reshape(8, 2, ROWS, 1, LANES),
        lower_image,
        image_weights,
        anisotropy,
        damping,
    )
    out = pl.pallas_call(
        evolve,
        out_shape=jax.ShapeDtypeStruct((3, 8, 2, ROWS, 1, LANES), f32),
        in_specs=[vmem] * 4,
        out_specs=anywhere,
        scratch_shapes=[
            pltpu.VMEM((EXT, 2, 3) + tile, f32),
            pltpu.VMEM((EXT, 2, 3) + tile, f32),
            pltpu.VMEM((ROWS + 1, 2, 3) + tile, f32),
            pltpu.VMEM((ROWS + 1, 2, 3) + tile, f32),
            pltpu.VMEM((ROWS, 3, 2, 3) + tile, f32),
            pltpu.VMEM((ROWS, 2, 3) + tile, f32),
            pltpu.SemaphoreType.DMA,
        ],
    )(*[pltpu.with_memory_space_constraint(p, pltpu.VMEM) for p in parts])
    return out.reshape(magnetization.shape)


def solution(mesh):
    placed = (P("img", None, None, "gy", "gx"), P(), P(), P(None, "gy", "gx"), P(), P())
    shape = (mesh.shape["img"], mesh.shape["gx"], mesh.shape["gy"])
    return jax.shard_map(
        lambda *args: body(shape, *args),
        mesh=mesh,
        in_specs=placed,
        out_specs=P("img", None, None, "gy", "gx"),
        check_vma=False,
    )
```
